32 devices in a mesh: snap: 4 (over z), cell: 8 (over y, x, core).
Axes of the slice: x: 2, y: 2, z: 4, core: 2. Of those that a mesh axis runs over, the one named last changes fastest.
Arguments:
- pressure: float32 [8320, 16384], P('snap', 'cell'), may hold values from -180 to 180
- block_starts: int32 [64], replicated, may hold values from 0 to 8064, as said below
- retained_bins: int32 [64], replicated, may hold values from 0 to 127
Outputs:
- spectral_gram: float32 [64, 2, 64, 64], P('snap')
The draws below stay inside these ranges and needn't reach their ends.
Inputs may be any that keep to these rules, and one draw needn't show every extreme that they name: `block_starts`: the 64 values are distinct multiples of 128.
All inputs are finite; a program needn't handle non-finite values.
Results may differ from the reference program's by a relative error of at most 0.0003.
Values sent between devices are 32-bit elements; how exact they have to be, the bound alone decides.
A program may use at most 128 MiB of HBM per device.

```python
import jax
import jax.numpy as jnp
from jax import lax

NFFT = 256
HOP = 128
BLOCKS = 64
SNAPS = 8320
K = 64
CELL_DEV = 2048
CELLS = 16384


def draw_pressure(key, part):
    subkeys = jax.random.split(key, 3)
    cells = jnp.arange(CELLS, dtype=jnp.float32)
    cell_scale = jnp.exp(jnp.log(10.0) * cells / CELLS) * jax.random.uniform(subkeys[1], (CELLS,), minval=0.7, maxval=1.4)
    time_scale = jnp.exp(jax.random.uniform(subkeys[2], (SNAPS, 1), minval=jnp.log(0.4), maxval=jnp.log(2.5)))
    values = jax.random.truncated_normal(subkeys[0], -5.0, 5.0, (SNAPS, CELLS))
    return (values * time_scale * cell_scale[None, :]).astype(jnp.float32)


def draw_block_starts(key, part):
    order = jax.random.permutation(jax.random.fold_in(key, 17), BLOCKS)
    return (order * HOP).astype(jnp.int32)


def place_ends(drawn, stream_key, low, top_value):
    longest = drawn.shape.index(max(drawn.shape))
    spots = []
    for shift in (0, 1):
        where = [jax.random.randint(jax.random.fold_in(stream_key, axis), (), 0, length) for axis, length in enumerate(drawn.shape)]
        where[longest] = (where[longest] + shift) % drawn.shape[longest]
        spots.append(tuple(where))
    return drawn.at[spots[0]].set(low).at[spots[1]].set(top_value)


def setup_inputs(seed: int = 0) -> dict:
    splits = jax.random.split(jax.random.key(seed), 4)
    return {
        "pressure": draw_pressure(jax.random.fold_in(splits[3], 71), 0),
        "block_starts": draw_block_starts(jax.random.fold_in(splits[3], 71), 0),
        "retained_bins": place_ends(jax.random.randint(splits[2], (K,), 0, HOP), jax.random.fold_in(splits[2], 1), 0, HOP - 1).astype(jnp.int32),
    }


def make_table(retained_bins):
    offsets = jnp.arange(NFFT, dtype=jnp.int32)
    window = 0.5 - 0.5 * jnp.cos(2.0 * jnp.pi * offsets.astype(jnp.float32) / NFFT)
    norm_factor = 1.0 / jnp.sqrt(jnp.sum(window * window))
    phase_steps = retained_bins[:, None] * offsets[None, :] % NFFT
    angles = 2.0 * jnp.pi * phase_steps.astype(jnp.float32) / NFFT
    wave_table = jnp.stack([window * norm_factor * jnp.cos(angles), -window * norm_factor * jnp.sin(angles)], 1)
    return wave_table.reshape(2 * retained_bins.shape[0], NFFT)

def reference(pressure, block_starts, retained_bins):
    wave_table = make_table(retained_bins)
    block_count = CELLS // CELL_DEV

    def accumulate(total_gram, block_number):
        column_block = lax.dynamic_slice_in_dim(pressure, (block_number * CELL_DEV).astype(jnp.int32), CELL_DEV, 1)
        windows = jax.vmap(lambda anchor: lax.dynamic_slice_in_dim(column_block, anchor.astype(jnp.int32), NFFT, 0))(block_starts)
        spectra = jnp.einsum('rt,btc->rbc', wave_table, windows, precision=lax.Precision.HIGHEST)
        stacked = spectra.reshape(K, 2 * BLOCKS, CELL_DEV)
        products = jnp.einsum('kbc,kdc->kbd', stacked, stacked, precision=lax.Precision.HIGHEST)
        return (total_gram + products, None)
    initial = jnp.zeros((K, 2 * BLOCKS, 2 * BLOCKS), jnp.float32)
    total_gram, unused = lax.scan(accumulate, initial, jnp.arange(block_count, dtype=jnp.int32))
    real_part = total_gram[:, :BLOCKS, :BLOCKS] + total_gram[:, BLOCKS:, BLOCKS:]
    imag_part = total_gram[:, :BLOCKS, BLOCKS:] - total_gram[:, BLOCKS:, :BLOCKS]
    return jnp.stack([real_part, imag_part], 1) / CELLS
```

```python
import functools

import jax
import jax.numpy as jnp
from jax import lax
from jax.experimental import pallas as pl
from jax.experimental.pallas import tpu as pltpu
from jax.sharding import PartitionSpec as P

NFFT = 256
LANES = 128
AHEAD = 3
MESH = pl.DeviceIdType.MESH


def make_table(bins):
    offsets = lax.broadcasted_iota(jnp.int32, (NFFT, bins.shape[1]), 0)
    window = 0.5 - 0.5 * jnp.cos(2.0 * jnp.pi * offsets.astype(jnp.float32) / NFFT)
    norm_factor = 1.0 / jnp.sqrt(jnp.sum(window * window, axis=0, keepdims=True))
    phase_steps = (bins * offsets) & (NFFT - 1)
    angles = 2.0 * jnp.pi * phase_steps.astype(jnp.float32) / NFFT
    return jnp.concatenate([window * norm_factor * jnp.cos(angles), -window * norm_factor * jnp.sin(angles)], 1)


def repeat(count, unroll, step):
    def body(turn, carry):
        for extra in range(unroll):
            step(turn * unroll + extra)
        return carry

    lax.fori_loop(0, count // unroll, body, 0)
    for rest in range(count // unroll * unroll, count):
        step(rest)


def pipeline_kernel(snap_count, cell_count, chunks, wide, kept_count, blocks, scale, pressure_ref, bins_ref, starts_ref, out_ref, held, half_held,
                    spectra, half_spectra, landed, grams, table_rows, table_parts, turns, sides, packed, cell_slots, own_cells, near_slots, lent_slots, far_sums, far_slot, own_part,
                    gathered, late_slots, own_sem, send_sem, recv_sem, half_own, half_send, half_recv, halo_send, halo_recv, keep_sem,
                    spec_send, spec_recv, cell_send, cell_recv, near_send, near_recv, lent_send, lent_recv, forward_send, forward_recv,
                    gather_send, gather_recv, late_send, late_recv, line_sem, flip_sem):
    my_snap, my_cell = lax.axis_index("snap"), lax.axis_index("cell")
    row_count = pressure_ref.shape[0]
    half_count = snap_count // 2
    my_half = my_snap // half_count
    half_start = my_half * half_count
    half_len = NFFT // 2
    half_rows = half_count * row_count
    half_blocks = blocks // 2
    halo = half_rows % half_len
    last = chunks - 1
    rows_out = 2 * kept_count
    groups = kept_count // snap_count // 2
    group_rows = 4 * half_blocks
    early_rows = groups * blocks // cell_count
    near = [half_start + lax.rem(my_snap + step, half_count) for step in range(1, half_count)]
    far = [half_count - my_half + step * (1 - 2 * my_half) for step in range(half_count)]
    others = near + far
    outer = my_half * (snap_count - 1)
    at_end = my_snap == outer

    def cell_peer(step):
        return lax.rem(my_cell + step, cell_count)

    bits = cell_count.bit_length() - 1

    def cell_flip(bit):
        return my_cell + 2 ** bit * (1 - 2 * lax.rem(my_cell // 2 ** bit, 2))

    def along(step):
        pl.when(my_snap > 0)(lambda: step(my_snap - 1, 1))
        pl.when(my_snap < snap_count - 1)(lambda: step(my_snap + 1, 0))

    barrier = pltpu.get_barrier_semaphore()
    along(lambda snap, side: pl.semaphore_signal(barrier, inc=1, device_id=(snap, my_cell), device_id_type=MESH))
    for bit in range(bits):
        pl.semaphore_signal(barrier, inc=1, device_id=(my_snap, cell_flip(bit)), device_id_type=MESH)
    pl.semaphore_wait(barrier, bits + jnp.minimum(my_snap, 1) + jnp.minimum(snap_count - 1 - my_snap, 1))

    def remote(source, target, send, recv, snap, cell):
        return pltpu.make_async_remote_copy(
            src_ref=source, dst_ref=target, send_sem=send, recv_sem=recv, device_id=(snap, cell), device_id_type=MESH
        )

    def columns(chunk, owner):
        return pl.ds(pl.multiple_of((chunk * snap_count + owner) * wide, wide), wide)

    def rows_of(source):
        return pl.ds(pl.multiple_of(source * row_count, 8), row_count)

    def sending(chunk, peer):
        return remote(pressure_ref.at[:, columns(chunk, peer)], held.at[chunk, rows_of(my_snap)],
                      send_sem.at[chunk, peer], recv_sem.at[chunk, my_snap], peer, my_cell)

    def arriving(chunk, peer):
        return remote(pressure_ref.at[:, columns(chunk, peer)], held.at[chunk, rows_of(peer)],
                      send_sem.at[chunk, peer], recv_sem.at[chunk, peer], peer, my_cell)

    def keeping(chunk):
        return pltpu.make_async_copy(pressure_ref.at[:, columns(chunk, my_snap)], held.at[chunk, rows_of(my_snap)], own_sem.at[chunk])

    def half_columns(peer, side):
        return columns(last, lax.rem(peer, half_count) + side * half_count)

    def half_place(source):
        return pl.ds(pl.multiple_of(my_half * halo + lax.rem(source, half_count) * row_count, 8), row_count)

    def half_sending(peer, side):
        return remote(pressure_ref.at[:, half_columns(peer, side)], half_held.at[side, half_place(my_snap)],
                      half_send.at[peer, side], half_recv.at[my_snap, side], peer, my_cell)

    def half_arriving(peer, side):
        return remote(pressure_ref.at[:, half_columns(my_snap, side)], half_held.at[side, half_place(peer)],
                      half_send.at[peer, side], half_recv.at[peer, side], peer, my_cell)

    def half_keeping(side):
        return pltpu.make_async_copy(pressure_ref.at[:, half_columns(my_snap, side)], half_held.at[side, half_place(my_snap)],
                                     half_own.at[side])

    def halo_sending(peer, side, half):
        first, place = (row_count - halo, 0) if half == 0 else (0, half_rows)
        return remote(pressure_ref.at[pl.ds(first, halo), half_columns(peer, side)], half_held.at[side, pl.ds(place, halo)],
                      halo_send.at[peer, side], halo_recv.at[side], peer, my_cell)

    def spectra_rows(owner, group):
        return pl.ds(pl.multiple_of((owner * groups + group) * group_rows, group_rows), group_rows)

    def spectra_sending(group, peer):
        return remote(half_spectra.at[:, spectra_rows(peer, group)], landed.at[my_snap, :, pl.ds(group * group_rows, group_rows)],
                      spec_send.at[group, peer], spec_recv.at[group, my_snap], peer, my_cell)

    def spectra_arriving(group, peer):
        return remote(half_spectra.at[:, spectra_rows(peer, group)], landed.at[peer, :, pl.ds(group * group_rows, group_rows)],
                      spec_send.at[group, peer], spec_recv.at[group, peer], peer, my_cell)

    def spectra_keeping():
        own = pl.ds(pl.multiple_of(my_snap * groups * group_rows, group_rows), groups * group_rows)
        return pltpu.make_async_copy(half_spectra.at[:, own], landed.at[my_snap], keep_sem.at[0])

    def at_middle(half, step):
        @pl.when(my_snap == half_count - 1 + half)
        def _():
            for peer in far:
                for side in range(2):
                    step(halo_sending(peer, side, half))

    at_cut = my_snap == half_count - 1 + my_half

    @pl.when(at_cut)
    def _():
        sending(0, far[0]).start()

    for turn in range(snap_count - 2):
        along(lambda snap, side, turn=turn: pl.semaphore_signal(
            line_sem.at[turn, side], inc=1, device_id=(snap, my_cell), device_id_type=MESH))
        along(lambda snap, side, turn=turn: pl.semaphore_wait(line_sem.at[turn, 1 - side], 1))
    for bit in range(bits):
        pl.semaphore_signal(flip_sem.at[bit], inc=1, device_id=(my_snap, cell_flip(bit)), device_id_type=MESH)
        pl.semaphore_wait(flip_sem.at[bit], 1)

    for half in range(2):
        at_middle(half, lambda copy: copy.start())
    for side in range(2):
        for peer in near:
            half_sending(peer, side).start()
        half_keeping(side).start()
    for chunk in range(last):
        for peer in near:
            sending(chunk, peer).start()
        keeping(chunk).start()
    def send_far(begun):
        for chunk in range(last):
            for peer in far[begun if chunk == 0 else 0:]:
                sending(chunk, peer).start()

    pl.when(at_cut)(lambda: send_far(1))

    table = make_table(bins_ref[...]).T
    for side in range(NFFT // LANES):
        for part in range(2):
            for slot in range(2 * snap_count):
                first = part * kept_count + slot * groups
                place = slot // 2 * 4 * groups + slot % 2 * 2 + part
                table_rows[side, pl.ds(place, groups, stride=4), :] = table[first:first + groups, side * LANES:(side + 1) * LANES]
    table = jnp.concatenate([table_rows[side] for side in range(NFFT // LANES)], 1)
    coarse = table.astype(jnp.bfloat16)
    table_parts[:rows_out] = coarse
    table_parts[rows_out:] = (table - coarse.astype(jnp.float32)).astype(jnp.bfloat16)

    lanes = 2 * blocks
    starts = jnp.concatenate([starts_ref[...]] * 2, 1).astype(jnp.float32)
    across = jnp.broadcast_to(starts, (lanes, lanes))
    down = across.T
    sides[0] = down
    sides[1] = across
    row = lax.broadcasted_iota(jnp.int32, (lanes, lanes), 0)
    lane = lax.broadcasted_iota(jnp.int32, (lanes, lanes), 1)
    same_side = (row < blocks) == (lane < blocks)
    row_slot = (half_len * jnp.where(row < blocks, row, row - blocks)).astype(jnp.float32)
    lane_slot = (half_len * jnp.where(lane < blocks, lane, lane - blocks)).astype(jnp.float32)
    turns[0] = jnp.where(same_side & (down == lane_slot), 1.0, 0.0).astype(jnp.bfloat16)
    turns[1] = jnp.where(same_side & (across == row_slot), 1.0, 0.0).astype(jnp.bfloat16)

    def split(data):
        coarse = data.astype(jnp.bfloat16)
        return coarse, (data - coarse.astype(jnp.float32)).astype(jnp.bfloat16)

    def thirds(data):
        coarse, rest = split(data)
        middle = data - coarse.astype(jnp.float32)
        return [coarse, rest, (middle - rest.astype(jnp.float32)).astype(jnp.bfloat16)]

    def reorder(tile):
        left = jnp.dot(turns[0, :blocks, :blocks], jnp.concatenate(thirds(tile), 1), preferred_element_type=jnp.float32)
        tile = (left[:, :lanes] + left[:, lanes:2 * lanes]) + left[:, 2 * lanes:]
        right = jnp.dot(jnp.concatenate(thirds(tile), 0), turns[1], preferred_element_type=jnp.float32)
        return (right[:blocks] + right[blocks:2 * blocks]) + right[2 * blocks:]

    def waves(windows):
        data_coarse, data_fine = split(jnp.concatenate(windows, 1))
        both = jnp.dot(table_parts[...], data_coarse, preferred_element_type=jnp.float32)
        rest = jnp.dot(table_parts[:rows_out], data_fine, preferred_element_type=jnp.float32)
        result = both[:rows_out] + (both[rows_out:] + rest)
        return [result[:, i * wide:(i + 1) * wide] for i in range(len(windows))]

    def window_rows(block):
        return pl.ds(pl.multiple_of(block * half_len, half_len), NFFT)

    def transform(chunk, first, count):
        def spread(block, width):
            results = waves([held[chunk, window_rows(block + i), :] for i in range(width)])
            for i, result in enumerate(results):
                spectra[pl.ds(block + i, rows_out, stride=blocks), :] = result

        repeat(count // 2, 2, lambda step: spread(first + 2 * step, 2))
        if count % 2:
            spread(first + count - 1, 1)

    def half_transform(block):
        results = waves([half_held[side, window_rows(block), :] for side in range(2)])
        for side, result in enumerate(results):
            half_spectra[side, pl.ds(block, rows_out, stride=half_blocks), :] = result

    for side in range(2):
        half_keeping(side).wait()
        for peer in near:
            half_arriving(peer, side).wait_recv()
        halo_sending(my_snap, side, 0).wait_recv()
    repeat(half_blocks, 2, half_transform)
    spectra_keeping().start()

    for peer in near:
        for group in range(groups):
            spectra_sending(group, peer).start()
    pl.when(jnp.logical_not(at_cut))(lambda: send_far(0))

    def send_spectra(group):
        for peer in reversed(far):
            spectra_sending(group, peer).start()

    for group in range(min(AHEAD, groups)):
        send_spectra(group)

    def gram_product(data):
        data_coarse, data_fine = split(data)
        right = jnp.concatenate([data_coarse, data_fine], 0)
        both = lax.dot_general(data_coarse, right, (((1,), (1,)), ((), ())), preferred_element_type=jnp.float32)
        cross = both[:, 2 * blocks:]
        return both[:, :2 * blocks] + (cross + cross.T)

    def chunk_product(place):
        return gram_product(spectra[pl.ds(pl.multiple_of(place * 2 * blocks, 2 * blocks), 2 * blocks), :])

    def complex_gram(whole):
        top, turned = whole[:blocks], pltpu.roll(whole[blocks:], blocks, 1)
        lane = lax.broadcasted_iota(jnp.int32, top.shape, 1)
        return jnp.where(lane < blocks, top + turned, top - turned)

    def pair_up(first, second):
        first, second = complex_gram(first), complex_gram(second)
        row = lax.broadcasted_iota(jnp.int32, first.shape, 0)
        lane = lax.broadcasted_iota(jnp.int32, first.shape, 1)
        left = jnp.where(row >= lane, first, pltpu.roll(first, blocks, 1))
        right = jnp.where(row >= lane - blocks, pltpu.roll(second, blocks, 1), second)
        return jnp.where(lane < blocks, left, right)

    high_start = -(-half_rows // half_len)
    low_count = (half_rows - NFFT) // half_len + 1
    for chunk in range(last):
        keeping(chunk).wait()
        for peer in near:
            arriving(chunk, peer).wait_recv()
        transform(chunk, my_half * high_start, low_count)
        for peer in far:
            arriving(chunk, peer).wait_recv()
        if chunk == last - 1:
            for group in range(AHEAD, min(2 * AHEAD, groups)):
                send_spectra(group)
        transform(chunk, low_count, high_start - low_count)
        transform(chunk, (1 - my_half) * high_start, low_count)
        if chunk < last - 1:
            def accumulate(place, chunk=chunk):
                grams[place] = chunk_product(place) if chunk == 0 else grams[place] + chunk_product(place)

            repeat(kept_count, 4, accumulate)

    def early_gram(place):
        return grams[place] + chunk_product(place) if last > 1 else chunk_product(place)

    def early_pack(pair):
        packed[pl.ds(pl.multiple_of(pair * blocks, blocks), blocks)] = pair_up(early_gram(2 * pair), early_gram(2 * pair + 1))

    def early_share(owner, cell):
        return pl.ds(pl.multiple_of(owner * groups * blocks + cell * early_rows, 8), early_rows)

    def scattering(owner, step):
        return remote(packed.at[early_share(owner, cell_peer(step))], cell_slots.at[step - 1, owner],
                      cell_send.at[step - 1, owner], cell_recv.at[step - 1, owner], my_snap, cell_peer(step))

    def near_exchanging(peer):
        return remote(own_cells.at[peer], near_slots.at[lax.rem(my_snap, half_count)], near_send.at[peer],
                      near_recv.at[lax.rem(my_snap, half_count)], peer, my_cell)

    def near_exchanged(peer):
        return remote(own_cells.at[peer], near_slots.at[lax.rem(peer, half_count)], near_send.at[peer],
                      near_recv.at[lax.rem(peer, half_count)], peer, my_cell)

    def lending(source):
        place = lax.rem(source, half_count)
        return remote(own_cells.at[pl.ds(half_count - half_start, half_count)], lent_slots.at[place], lent_send.at[0],
                      lent_recv.at[place], outer, my_cell)

    def forwarding(peer):
        return remote(far_sums.at[lax.rem(peer, half_count)], far_slot, forward_send.at[peer], forward_recv.at[0], peer, my_cell)

    def gather_rows(cell):
        return pl.ds(pl.multiple_of(cell * early_rows, 8), early_rows)

    def gathering(step):
        return remote(own_part, gathered.at[gather_rows(my_cell)], gather_send.at[step - 1], gather_recv.at[my_cell], my_snap, cell_peer(step))

    def gather_arriving(step):
        return remote(own_part, gathered.at[gather_rows(cell_peer(step))], gather_send.at[step - 1], gather_recv.at[cell_peer(step)],
                      my_snap, cell_peer(step))

    for owner in range(snap_count):
        repeat(groups, 2, lambda pair, owner=owner: early_pack(owner * groups + pair))
        for step in range(1, cell_count):
            scattering(owner, step).start()

    def early_exchange():
        for owner in range(snap_count):
            total = packed[early_share(owner, my_cell)]
            for step in range(1, cell_count):
                scattering(owner, step).wait_recv()
                total = total + cell_slots[step - 1, owner]
            own_cells[owner] = total
        for peer in near:
            near_exchanging(peer).start()
        pl.when(jnp.logical_not(at_end))(lambda: lending(my_snap).start())

    def early_forward():
        @pl.when(at_end)
        def _():
            total = own_cells[pl.ds(half_count - half_start, half_count)]
            for peer in near:
                lending(peer).wait_recv()
                total = total + lent_slots[lax.rem(peer, half_count)]
            far_sums[...] = total
            for peer in far:
                forwarding(peer).start()

    def early_gather():
        part = own_cells[my_snap]
        for peer in near:
            near_exchanged(peer).wait_recv()
            part = part + near_slots[lax.rem(peer, half_count)]
        forwarding(my_snap).wait_recv()
        part = part + far_slot[...]
        own_part[...] = part
        for step in range(1, cell_count):
            gathering(step).start()
        gathered[gather_rows(my_cell)] = part

    def early_collect():
        for step in range(1, cell_count):
            gather_arriving(step).wait_recv()

    def late_gram(group, member):
        sets = []
        for place in range(half_count):
            for side in range(2):
                rows = [
                    landed[half * half_count + place, side, pl.ds(group * group_rows + (2 * member + part) * half_blocks, half_blocks), :]
                    for part in range(2)
                    for half in range(2)
                ]
                sets.append(jnp.concatenate(rows, 0))
        return gram_product(jnp.concatenate(sets, 1))

    def late_sending(group, step):
        return remote(late_slots.at[group, my_cell], late_slots.at[group, my_cell], late_send.at[group, step - 1],
                      late_recv.at[group, my_cell], my_snap, cell_peer(step))

    def late_arriving(group, step):
        return remote(late_slots.at[group, my_cell], late_slots.at[group, cell_peer(step)], late_send.at[group, step - 1],
                      late_recv.at[group, cell_peer(step)], my_snap, cell_peer(step))

    def late_share(group):
        for peer in others:
            spectra_arriving(group, peer).wait_recv()
        if 2 * AHEAD <= group + AHEAD < groups:
            send_spectra(group + AHEAD)
        late_slots[group, my_cell] = pair_up(late_gram(group, 0), late_gram(group, 1))
        for step in range(1, cell_count):
            late_sending(group, step).start()

    def late_sum(group):
        for step in range(1, cell_count):
            late_arriving(group, step).wait_recv()
        total = late_slots[group, 0]
        for cell in range(1, cell_count):
            total = total + late_slots[group, cell]
        total = (total + gathered[pl.ds(group * blocks, blocks)]) * scale
        tile = reorder(total)
        turned = tile.T
        rolled = pltpu.roll(tile, blocks, 1)
        before, after = sides[0, :blocks, :blocks], sides[1, :blocks, :blocks]
        for member in range(2):
            straight = (tile if member == 0 else rolled)[:, :blocks]
            mirrored = turned[member * blocks:(member + 1) * blocks]
            place = member * groups + group
            out_ref[place, 0] = jnp.where(before >= after, straight, mirrored)
            out_ref[place, 1] = jnp.where(before == after, 0.0, jnp.where(before >= after, -mirrored, straight))

    spectra_keeping().wait()
    def finish_late(done):
        for group in done:
            for peer in far:
                spectra_sending(group, peer).wait_send()
            for step in range(1, cell_count):
                late_sending(group, step).wait_send()

    def finish_early():
        for half in range(2):
            at_middle(half, lambda copy: copy.wait_send())
        for peer in near:
            for side in range(2):
                half_sending(peer, side).wait_send()
            for group in range(groups):
                spectra_sending(group, peer).wait_send()
        for chunk in range(last):
            for peer in others:
                sending(chunk, peer).wait_send()
        for step in range(1, cell_count):
            gathering(step).wait_send()
            for owner in range(snap_count):
                scattering(owner, step).wait_send()
        for peer in near:
            near_exchanging(peer).wait_send()
        pl.when(jnp.logical_not(at_end))(lambda: lending(my_snap).wait_send())

        @pl.when(at_end)
        def _():
            for peer in far:
                forwarding(peer).wait_send()

    ended = max(groups - 2, 0)
    ready = min(5, groups - 1)
    steps = {}
    for turn, step in ((0, early_exchange), (1, early_forward), (3, early_gather), (ready, early_collect)):
        steps.setdefault(min(turn, groups - 1), []).append(step)
    for group in range(groups):
        late_share(group)
        for step in steps.get(group, []):
            step()
        if group >= ready:
            for done in range(0 if group == ready else group - 1, group):
                late_sum(done)
        if group == max(groups - 2, 0):
            finish_late(range(ended))
        if group == max(groups - 2, ready):
            finish_early()
    late_sum(groups - 1)

    finish_late(range(ended, groups))


def pipelined_grams(pressure, block_starts, retained_bins, snap_count, cell_count, blocks):
    row_count, width_local = pressure.shape
    wide = LANES
    chunks = width_local // snap_count // wide
    kept_count = retained_bins.shape[0]
    groups = kept_count // snap_count // 2
    early_rows = groups * blocks // cell_count
    lanes = 2 * blocks
    half_len = NFFT // 2
    half_rows = snap_count // 2 * row_count
    halo = half_rows % half_len
    assert cell_count & (cell_count - 1) == 0 and snap_count > 2
    assert halo == half_len // 2 and halo <= row_count and blocks % 2 == 0 and snap_count % 2 == 0
    whole_vmem = pl.BlockSpec(memory_space=pltpu.VMEM)
    scale = 1.0 / (width_local * cell_count)
    semaphores = pltpu.SemaphoreType.DMA
    return pl.pallas_call(
        functools.partial(pipeline_kernel, snap_count, cell_count, chunks, wide, kept_count, blocks, scale),
        out_shape=jax.ShapeDtypeStruct((2 * groups, 2, blocks, blocks), jnp.float32),
        in_specs=[pl.BlockSpec(memory_space=pl.ANY), whole_vmem, whole_vmem],
        out_specs=whole_vmem,
        scratch_shapes=[
            pltpu.VMEM((chunks - 1, snap_count * row_count, wide), jnp.float32),
            pltpu.VMEM((2, half_rows + halo, wide), jnp.float32),
            pltpu.VMEM((2 * kept_count * blocks, wide), jnp.float32),
            pltpu.VMEM((2, kept_count * blocks, wide), jnp.float32),
            pltpu.VMEM((snap_count, 2, 2 * groups * blocks, wide), jnp.float32),
            pltpu.VMEM((kept_count, lanes, lanes), jnp.float32),
            pltpu.VMEM((NFFT // LANES, 2 * kept_count, LANES), jnp.float32),
            pltpu.VMEM((4 * kept_count, NFFT), jnp.bfloat16),
            pltpu.VMEM((2, lanes, lanes), jnp.bfloat16),
            pltpu.VMEM((2, lanes, lanes), jnp.float32),
            pltpu.VMEM((snap_count * groups * blocks, lanes), jnp.float32),
            pltpu.VMEM((cell_count - 1, snap_count, early_rows, lanes), jnp.float32),
            pltpu.VMEM((snap_count, early_rows, lanes), jnp.float32),
            pltpu.VMEM((snap_count // 2, early_rows, lanes), jnp.float32),
            pltpu.VMEM((snap_count // 2, snap_count // 2, early_rows, lanes), jnp.float32),
            pltpu.VMEM((snap_count // 2, early_rows, lanes), jnp.float32),
            pltpu.VMEM((early_rows, lanes), jnp.float32),
            pltpu.VMEM((early_rows, lanes), jnp.float32),
            pltpu.VMEM((groups * blocks, lanes), jnp.float32),
            pltpu.VMEM((groups, cell_count, blocks, lanes), jnp.float32),
            semaphores((chunks,)),
            semaphores((chunks, snap_count)),
            semaphores((chunks, snap_count)),
            semaphores((2,)),
            semaphores((snap_count, 2)),
            semaphores((snap_count, 2)),
            semaphores((snap_count, 2)),
            semaphores((2,)),
            semaphores((1,)),
            semaphores((groups, snap_count)),
            semaphores((groups, snap_count)),
            semaphores((cell_count - 1, snap_count)),
            semaphores((cell_count - 1, snap_count)),
            semaphores((snap_count,)),
            semaphores((snap_count // 2,)),
            semaphores((1,)),
            semaphores((snap_count // 2,)),
            semaphores((snap_count,)),
            semaphores((1,)),
            semaphores((cell_count - 1,)),
            semaphores((cell_count,)),
            semaphores((groups, cell_count - 1)),
            semaphores((groups, cell_count)),
            pltpu.SemaphoreType.REGULAR((snap_count - 2, 2)),
            pltpu.SemaphoreType.REGULAR((cell_count.bit_length() - 1,)),
        ],
        compiler_params=pltpu.CompilerParams(collective_id=2, has_side_effects=True, vmem_limit_bytes=46 * 2**20),
    )(pressure, retained_bins.reshape(1, kept_count), block_starts.reshape(1, blocks))


def gather_kernel(snap_count, chunks, wide, kept_count, blocks, pressure_ref, bins_ref, out_ref, held, spectra, grams,
                  table_parts, own_sem, send_sem, recv_sem):
    my_snap, my_cell = lax.axis_index("snap"), lax.axis_index("cell")
    row_count = pressure_ref.shape[0]
    half_count = snap_count // 2
    my_half = my_snap // half_count
    half_len = NFFT // 2
    near = [my_half * half_count + lax.rem(my_snap + step, half_count) for step in range(1, half_count)]
    far = [(1 - my_half) * half_count + lax.rem(my_snap + step, half_count) for step in range(half_count)]

    barrier = pltpu.get_barrier_semaphore()
    for peer in near + far:
        pl.semaphore_signal(barrier, inc=1, device_id=(peer, my_cell), device_id_type=MESH)
    pl.semaphore_wait(barrier, snap_count - 1)

    def columns(chunk, owner):
        return pressure_ref.at[:, pl.ds(pl.multiple_of((chunk * snap_count + owner) * wide, wide), wide)]

    def landing(chunk, source):
        return held.at[chunk, pl.ds(pl.multiple_of(source * row_count, 8), row_count)]

    def sending(chunk, peer):
        return pltpu.make_async_remote_copy(
            src_ref=columns(chunk, peer),
            dst_ref=landing(chunk, my_snap),
            send_sem=send_sem.at[chunk, peer],
            recv_sem=recv_sem.at[chunk, my_snap],
            device_id=(peer, my_cell),
            device_id_type=MESH,
        )

    def arriving(chunk, peer):
        return pltpu.make_async_remote_copy(
            src_ref=columns(chunk, peer),
            dst_ref=landing(chunk, peer),
            send_sem=send_sem.at[chunk, peer],
            recv_sem=recv_sem.at[chunk, peer],
            device_id=(peer, my_cell),
            device_id_type=MESH,
        )

    def keeping(chunk):
        return pltpu.make_async_copy(columns(chunk, my_snap), landing(chunk, my_snap), own_sem.at[chunk])

    for chunk in range(chunks):
        for peer in near:
            sending(chunk, peer).start()
        keeping(chunk).start()
    for chunk in range(chunks):
        for peer in far:
            sending(chunk, peer).start()

    table = make_table(bins_ref[...]).T
    coarse = table.astype(jnp.bfloat16)
    rows_out = 2 * kept_count
    table_parts[:rows_out] = coarse
    table_parts[rows_out:] = (table - coarse.astype(jnp.float32)).astype(jnp.bfloat16)

    half_rows = snap_count * row_count // 2
    low_count = (half_rows - NFFT) // half_len + 1
    high_start = -(-half_rows // half_len)
    assert low_count == blocks - high_start

    def transform(chunk, first, count):
        def spread(block, width):
            data = jnp.concatenate(
                [held[chunk, pl.ds(pl.multiple_of((block + i) * half_len, half_len), NFFT), :] for i in range(width)], 1
            )
            data_coarse = data.astype(jnp.bfloat16)
            data_fine = (data - data_coarse.astype(jnp.float32)).astype(jnp.bfloat16)
            both = jnp.dot(table_parts[...], data_coarse, preferred_element_type=jnp.float32)
            rest = jnp.dot(table_parts[:rows_out], data_fine, preferred_element_type=jnp.float32)
            result = both[:rows_out] + (both[rows_out:] + rest)
            for i in range(width):
                spectra[pl.ds(block + i, rows_out, stride=blocks), :] = result[:, i * wide:(i + 1) * wide]

        repeat(count // 2, 2, lambda step: spread(first + 2 * step, 2))
        if count % 2:
            spread(first + count - 1, 1)

    def product(k):
        data = jnp.concatenate(
            [spectra[pl.ds(pl.multiple_of((k + part * kept_count) * blocks, blocks), blocks), :] for part in range(2)], 0
        )
        data_coarse = data.astype(jnp.bfloat16)
        data_fine = (data - data_coarse.astype(jnp.float32)).astype(jnp.bfloat16)
        right = jnp.concatenate([data_coarse, data_fine], 0)
        both = lax.dot_general(data_coarse, right, (((1,), (1,)), ((), ())), preferred_element_type=jnp.float32)
        cross = both[:, 2 * blocks:]
        return both[:, :2 * blocks] + (cross + cross.T)

    def complex_gram(k):
        whole = grams[k] + product(k) if chunks > 1 else product(k)
        top, turned = whole[:blocks], pltpu.roll(whole[blocks:], blocks, 1)
        lane = lax.broadcasted_iota(jnp.int32, top.shape, 1)
        return jnp.where(lane < blocks, top + turned, top - turned)

    for chunk in range(chunks):
        keeping(chunk).wait()
        for peer in near:
            arriving(chunk, peer).wait_recv()
        transform(chunk, my_half * high_start, low_count)
        for peer in far:
            arriving(chunk, peer).wait_recv()
        transform(chunk, low_count, high_start - low_count)
        transform(chunk, (1 - my_half) * high_start, low_count)
        if chunk < chunks - 1:
            def accumulate(k, chunk=chunk):
                grams[k] = product(k) if chunk == 0 else grams[k] + product(k)

            repeat(kept_count, 4, accumulate)

    pairs = kept_count // snap_count // 2

    def finish(place):
        k = place // pairs * (2 * pairs) + lax.rem(place, pairs)
        first, second = complex_gram(k), complex_gram(k + pairs)
        row = lax.broadcasted_iota(jnp.int32, first.shape, 0)
        lane = lax.broadcasted_iota(jnp.int32, first.shape, 1)
        left = jnp.where(row >= lane, first, pltpu.roll(first, blocks, 1))
        right = jnp.where(row >= lane - blocks, pltpu.roll(second, blocks, 1), second)
        return jnp.where(lane < blocks, left, right)

    def write(place):
        out_ref[place] = finish(place)

    repeat(kept_count // 2, 2, write)
    for chunk in range(chunks):
        for peer in near + far:
            sending(chunk, peer).wait_send()


def local_grams(pressure, retained_bins, snap_count, blocks):
    row_count, width_local = pressure.shape
    wide = LANES
    chunks = width_local // snap_count // wide
    kept_count = retained_bins.shape[0]
    whole_vmem = pl.BlockSpec(memory_space=pltpu.VMEM)
    return pl.pallas_call(
        functools.partial(gather_kernel, snap_count, chunks, wide, kept_count, blocks),
        out_shape=jax.ShapeDtypeStruct((kept_count // 2, blocks, 2 * blocks), jnp.float32),
        in_specs=[pl.BlockSpec(memory_space=pl.ANY), whole_vmem],
        out_specs=whole_vmem,
        scratch_shapes=[
            pltpu.VMEM((chunks, snap_count * row_count, wide), jnp.float32),
            pltpu.VMEM((2 * kept_count * blocks, wide), jnp.float32),
            pltpu.VMEM((kept_count, 2 * blocks, 2 * blocks), jnp.float32),
            pltpu.VMEM((4 * kept_count, NFFT), jnp.bfloat16),
            pltpu.SemaphoreType.DMA((chunks,)),
            pltpu.SemaphoreType.DMA((chunks, snap_count)),
            pltpu.SemaphoreType.DMA((chunks, snap_count)),
        ],
        compiler_params=pltpu.CompilerParams(collective_id=1, has_side_effects=True),
    )(pressure, retained_bins.reshape(1, kept_count))


def reduce_kernel(snap_count, cell_count, scale, gram_ref, out_ref, cell_slots, own_cells, snap_slots, own_part, gathered,
                  cell_send, cell_recv, snap_send, snap_recv, gather_send, gather_recv):
    my_snap, my_cell = lax.axis_index("snap"), lax.axis_index("cell")

    def cell_peer(step):
        return lax.rem(my_cell + step, cell_count)

    def snap_peer(step):
        return lax.rem(my_snap + step, snap_count)

    barrier = pltpu.get_barrier_semaphore()
    for step in range(1, cell_count):
        pl.semaphore_signal(barrier, inc=1, device_id=(my_snap, cell_peer(step)), device_id_type=MESH)
    for step in range(1, snap_count):
        pl.semaphore_signal(barrier, inc=1, device_id=(snap_peer(step), my_cell), device_id_type=MESH)
    pl.semaphore_wait(barrier, cell_count + snap_count - 2)

    scatters = [
        pltpu.make_async_remote_copy(
            src_ref=gram_ref.at[:, cell_peer(step)],
            dst_ref=cell_slots.at[step - 1],
            send_sem=cell_send.at[step - 1],
            recv_sem=cell_recv.at[step - 1],
            device_id=(my_snap, cell_peer(step)),
            device_id_type=MESH,
        )
        for step in range(1, cell_count)
    ]
    for copy in scatters:
        copy.start()
    total = gram_ref[:, my_cell]
    for step in range(1, cell_count):
        scatters[step - 1].wait_recv()
        total = total + cell_slots[step - 1]
    own_cells[...] = total

    exchanges = [
        pltpu.make_async_remote_copy(
            src_ref=own_cells.at[snap_peer(step)],
            dst_ref=snap_slots.at[step - 1],
            send_sem=snap_send.at[step - 1],
            recv_sem=snap_recv.at[step - 1],
            device_id=(snap_peer(step), my_cell),
            device_id_type=MESH,
        )
        for step in range(1, snap_count)
    ]
    for copy in exchanges:
        copy.start()
    part = own_cells[my_snap]
    for step in range(1, snap_count):
        exchanges[step - 1].wait_recv()
        part = part + snap_slots[step - 1]
    own_part[...] = part * scale

    gathers = [
        pltpu.make_async_remote_copy(
            src_ref=own_part,
            dst_ref=gathered.at[my_cell],
            send_sem=gather_send.at[step - 1],
            recv_sem=gather_recv.at[step - 1],
            device_id=(my_snap, cell_peer(step)),
            device_id_type=MESH,
        )
        for step in range(1, cell_count)
    ]
    for copy in gathers:
        copy.start()
    out_ref[my_cell] = own_part[...]
    for step in range(1, cell_count):
        gathers[step - 1].wait_recv()
        source = lax.rem(my_cell + cell_count - step, cell_count)
        out_ref[source] = gathered[source]
    for copy in scatters + exchanges + gathers:
        copy.wait_send()


def reduce_grams(packed, scale):
    snap_count, cell_count, rows, lanes = packed.shape
    whole_vmem = pl.BlockSpec(memory_space=pltpu.VMEM)
    return pl.pallas_call(
        functools.partial(reduce_kernel, snap_count, cell_count, scale),
        out_shape=jax.ShapeDtypeStruct((cell_count, rows, lanes), jnp.float32),
        in_specs=[whole_vmem],
        out_specs=whole_vmem,
        scratch_shapes=[
            pltpu.VMEM((cell_count - 1, snap_count, rows, lanes), jnp.float32),
            pltpu.VMEM((snap_count, rows, lanes), jnp.float32),
            pltpu.VMEM((snap_count - 1, rows, lanes), jnp.float32),
            pltpu.VMEM((rows, lanes), jnp.float32),
            pltpu.VMEM((cell_count, rows, lanes), jnp.float32),
            pltpu.SemaphoreType.DMA((cell_count - 1,)),
            pltpu.SemaphoreType.DMA((cell_count - 1,)),
            pltpu.SemaphoreType.DMA((snap_count - 1,)),
            pltpu.SemaphoreType.DMA((snap_count - 1,)),
            pltpu.SemaphoreType.DMA((cell_count - 1,)),
            pltpu.SemaphoreType.DMA((cell_count - 1,)),
        ],
        compiler_params=pltpu.CompilerParams(collective_id=0, has_side_effects=True),
    )(packed)


def on_device(pressure, block_starts, retained_bins):
    snap_count = lax.axis_size("snap")
    row_count, width_local = pressure.shape
    kept_count = retained_bins.shape[0]
    blocks = block_starts.shape[0]
    lower = jnp.arange(blocks)[:, None] >= jnp.arange(blocks)[None, :]
    cell_count = lax.axis_size("cell")
    pairs = kept_count // snap_count // 2
    if pairs * blocks % (8 * cell_count) == 0 and width_local // snap_count // LANES > 1:
        return pipelined_grams(pressure, block_starts, retained_bins, snap_count, cell_count, blocks)
    halves = local_grams(pressure, retained_bins, snap_count, blocks)
    packed = halves.reshape(snap_count, cell_count, pairs * blocks // cell_count, 2 * blocks)
    reduced = reduce_grams(packed, 1.0 / (width_local * cell_count))
    paired = reduced.reshape(pairs, blocks, 2 * blocks)
    joined = jnp.concatenate([paired[:, :, :blocks], paired[:, :, blocks:]], 0)
    mirrored = joined.transpose(0, 2, 1)
    diagonal = jnp.eye(blocks, dtype=bool)
    own_real = jnp.where(lower, joined, mirrored)
    own_imag = jnp.where(diagonal, 0.0, jnp.where(lower, -mirrored, joined))
    own_block = jnp.stack([own_real, own_imag], 1)
    order = (block_starts[:, None] // (NFFT // 2) == jnp.arange(blocks)[None, :]).astype(jnp.float32)
    turned = jnp.einsum("kpij,dj->kpid", own_block, order, precision=lax.Precision.HIGHEST)
    return jnp.einsum("bi,kpid->kpbd", order, turned, precision=lax.Precision.HIGHEST)


def solution(mesh):
    placed = (P("snap", "cell"), P(), P())
    return jax.shard_map(
        on_device,
        mesh=mesh,
        in_specs=placed,
        out_specs=P("snap", None, None, None),
        check_vma=False,
    )
```

```python
import functools

import jax
import jax.numpy as jnp
from jax import lax
from jax.experimental import pallas as pl
from jax.experimental.pallas import tpu as pltpu
from jax.sharding import PartitionSpec as P

NFFT = 256
LANES = 128
AHEAD = 3
MESH = pl.DeviceIdType.MESH


def make_table(bins):
    offsets = lax.broadcasted_iota(jnp.int32, (NFFT, bins.shape[1]), 0)
    window = 0.5 - 0.5 * jnp.cos(2.0 * jnp.pi * offsets.astype(jnp.float32) / NFFT)
    norm_factor = 1.0 / jnp.sqrt(jnp.sum(window * window, axis=0, keepdims=True))
    phase_steps = (bins * offsets) & (NFFT - 1)
    angles = 2.0 * jnp.pi * phase_steps.astype(jnp.float32) / NFFT
    return jnp.concatenate([window * norm_factor * jnp.cos(angles), -window * norm_factor * jnp.sin(angles)], 1)


def repeat(count, unroll, step):
    def body(turn, carry):
        for extra in range(unroll):
            step(turn * unroll + extra)
        return carry

    lax.fori_loop(0, count // unroll, body, 0)
    for rest in range(count // unroll * unroll, count):
        step(rest)


def pipeline_kernel(snap_count, cell_count, chunks, wide, kept_count, blocks, scale, pressure_ref, index_ref, out_ref, held, half_held,
                    spectra, half_spectra, landed, grams, table_rows, table_parts, turns, sides, packed, cell_slots, own_cells, near_slots, lent_slots, far_sums, far_slot, own_part,
                    gathered, late_slots, own_sem, send_sem, recv_sem, half_own, half_send, half_recv, halo_send, halo_recv, keep_sem,
                    spec_send, spec_recv, cell_send, cell_recv, near_send, near_recv, lent_send, lent_recv, forward_send, forward_recv,
                    gather_send, gather_recv, late_send, late_recv, line_sem, flip_sem):
    my_snap, my_cell = lax.axis_index("snap"), lax.axis_index("cell")
    row_count = pressure_ref.shape[0]
    half_count = snap_count // 2
    my_half = my_snap // half_count
    half_start = my_half * half_count
    half_len = NFFT // 2
    half_rows = half_count * row_count
    half_blocks = blocks // 2
    halo = half_rows % half_len
    last = chunks - 1
    rows_out = 2 * kept_count
    groups = kept_count // snap_count // 2
    group_rows = 4 * half_blocks
    early_rows = groups * blocks // cell_count
    near = [half_start + lax.rem(my_snap + step, half_count) for step in range(1, half_count)]
    far = [half_count - my_half + step * (1 - 2 * my_half) for step in range(half_count)]
    others = near + far
    outer = my_half * (snap_count - 1)
    at_end = my_snap == outer

    def cell_peer(step):
        return lax.rem(my_cell + step, cell_count)

    bits = cell_count.bit_length() - 1

    def cell_flip(bit):
        return my_cell + 2 ** bit * (1 - 2 * lax.rem(my_cell // 2 ** bit, 2))

    def along(step):
        pl.when(my_snap > 0)(lambda: step(my_snap - 1, 1))
        pl.when(my_snap < snap_count - 1)(lambda: step(my_snap + 1, 0))

    barrier = pltpu.get_barrier_semaphore()
    along(lambda snap, side: pl.semaphore_signal(barrier, inc=1, device_id=(snap, my_cell), device_id_type=MESH))
    for bit in range(bits):
        pl.semaphore_signal(barrier, inc=1, device_id=(my_snap, cell_flip(bit)), device_id_type=MESH)
    pl.semaphore_wait(barrier, bits + jnp.minimum(my_snap, 1) + jnp.minimum(snap_count - 1 - my_snap, 1))

    def remote(source, target, send, recv, snap, cell):
        return pltpu.make_async_remote_copy(
            src_ref=source, dst_ref=target, send_sem=send, recv_sem=recv, device_id=(snap, cell), device_id_type=MESH
        )

    def columns(chunk, owner):
        return pl.ds(pl.multiple_of((chunk * snap_count + owner) * wide, wide), wide)

    def rows_of(source):
        return pl.ds(pl.multiple_of(source * row_count, 8), row_count)

    def sending(chunk, peer):
        return remote(pressure_ref.at[:, columns(chunk, peer)], held.at[chunk, rows_of(my_snap)],
                      send_sem.at[chunk, peer], recv_sem.at[chunk, my_snap], peer, my_cell)

    def arriving(chunk, peer):
        return remote(pressure_ref.at[:, columns(chunk, peer)], held.at[chunk, rows_of(peer)],
                      send_sem.at[chunk, peer], recv_sem.at[chunk, peer], peer, my_cell)

    def keeping(chunk):
        return pltpu.make_async_copy(pressure_ref.at[:, columns(chunk, my_snap)], held.at[chunk, rows_of(my_snap)], own_sem.at[chunk])

    def half_columns(peer, side):
        return columns(last, lax.rem(peer, half_count) + side * half_count)

    def half_place(source):
        return pl.ds(pl.multiple_of(my_half * halo + lax.rem(source, half_count) * row_count, 8), row_count)

    def half_sending(peer, side):
        return remote(pressure_ref.at[:, half_columns(peer, side)], half_held.at[side, half_place(my_snap)],
                      half_send.at[peer, side], half_recv.at[my_snap, side], peer, my_cell)

    def half_arriving(peer, side):
        return remote(pressure_ref.at[:, half_columns(my_snap, side)], half_held.at[side, half_place(peer)],
                      half_send.at[peer, side], half_recv.at[peer, side], peer, my_cell)

    def half_keeping(side):
        return pltpu.make_async_copy(pressure_ref.at[:, half_columns(my_snap, side)], half_held.at[side, half_place(my_snap)],
                                     half_own.at[side])

    def halo_sending(peer, side, half):
        first, place = (row_count - halo, 0) if half == 0 else (0, half_rows)
        return remote(pressure_ref.at[pl.ds(first, halo), half_columns(peer, side)], half_held.at[side, pl.ds(place, halo)],
                      halo_send.at[peer, side], halo_recv.at[side], peer, my_cell)

    def spectra_rows(owner, group):
        return pl.ds(pl.multiple_of((owner * groups + group) * group_rows, group_rows), group_rows)

    def spectra_sending(group, peer):
        return remote(half_spectra.at[:, spectra_rows(peer, group)], landed.at[my_snap, :, pl.ds(group * group_rows, group_rows)],
                      spec_send.at[group, peer], spec_recv.at[group, my_snap], peer, my_cell)

    def spectra_arriving(group, peer):
        return remote(half_spectra.at[:, spectra_rows(peer, group)], landed.at[peer, :, pl.ds(group * group_rows, group_rows)],
                      spec_send.at[group, peer], spec_recv.at[group, peer], peer, my_cell)

    def spectra_keeping():
        own = pl.ds(pl.multiple_of(my_snap * groups * group_rows, group_rows), groups * group_rows)
        return pltpu.make_async_copy(half_spectra.at[:, own], landed.at[my_snap], keep_sem.at[0])

    def at_middle(half, step):
        @pl.when(my_snap == half_count - 1 + half)
        def _():
            for peer in far:
                for side in range(2):
                    step(halo_sending(peer, side, half))

    at_cut = my_snap == half_count - 1 + my_half

    @pl.when(at_cut)
    def _():
        sending(0, far[0]).start()

    for turn in range(snap_count - 2):
        along(lambda snap, side, turn=turn: pl.semaphore_signal(
            line_sem.at[turn, side], inc=1, device_id=(snap, my_cell), device_id_type=MESH))
        along(lambda snap, side, turn=turn: pl.semaphore_wait(line_sem.at[turn, 1 - side], 1))
    for bit in range(bits):
        pl.semaphore_signal(flip_sem.at[bit], inc=1, device_id=(my_snap, cell_flip(bit)), device_id_type=MESH)
        pl.semaphore_wait(flip_sem.at[bit], 1)

    for half in range(2):
        at_middle(half, lambda copy: copy.start())
    for side in range(2):
        for peer in near:
            half_sending(peer, side).start()
        half_keeping(side).start()
    for chunk in range(last):
        for peer in near:
            sending(chunk, peer).start()
        keeping(chunk).start()
    def send_far(begun):
        for chunk in range(last):
            for peer in far[begun if chunk == 0 else 0:]:
                sending(chunk, peer).start()

    pl.when(at_cut)(lambda: send_far(1))

    table = make_table(index_ref[:1, :kept_count]).T
    for side in range(NFFT // LANES):
        for part in range(2):
            for slot in range(2 * snap_count):
                first = part * kept_count + slot * groups
                place = slot // 2 * 4 * groups + slot % 2 * 2 + part
                table_rows[side, pl.ds(place, groups, stride=4), :] = table[first:first + groups, side * LANES:(side + 1) * LANES]
    table = jnp.concatenate([table_rows[side] for side in range(NFFT // LANES)], 1)
    coarse = table.astype(jnp.bfloat16)
    table_parts[:rows_out] = coarse
    table_parts[rows_out:] = (table - coarse.astype(jnp.float32)).astype(jnp.bfloat16)

    lanes = 2 * blocks
    starts = jnp.concatenate([index_ref[1:, :blocks]] * 2, 1).astype(jnp.float32)
    across = jnp.broadcast_to(starts, (lanes, lanes))
    down = across.T
    sides[0] = down
    sides[1] = across
    row = lax.broadcasted_iota(jnp.int32, (lanes, lanes), 0)
    lane = lax.broadcasted_iota(jnp.int32, (lanes, lanes), 1)
    same_side = (row < blocks) == (lane < blocks)
    row_slot = (half_len * jnp.where(row < blocks, row, row - blocks)).astype(jnp.float32)
    lane_slot = (half_len * jnp.where(lane < blocks, lane, lane - blocks)).astype(jnp.float32)
    turns[0] = jnp.where(same_side & (down == lane_slot), 1.0, 0.0).astype(jnp.bfloat16)
    turns[1] = jnp.where(same_side & (across == row_slot), 1.0, 0.0).astype(jnp.bfloat16)

    def split(data):
        coarse = data.astype(jnp.bfloat16)
        return coarse, (data - coarse.astype(jnp.float32)).astype(jnp.bfloat16)

    def thirds(data):
        coarse, rest = split(data)
        middle = data - coarse.astype(jnp.float32)
        return [coarse, rest, (middle - rest.astype(jnp.float32)).astype(jnp.bfloat16)]

    def reorder(tile):
        left = jnp.dot(turns[0, :blocks, :blocks], jnp.concatenate(thirds(tile), 1), preferred_element_type=jnp.float32)
        tile = (left[:, :lanes] + left[:, lanes:2 * lanes]) + left[:, 2 * lanes:]
        right = jnp.dot(jnp.concatenate(thirds(tile), 0), turns[1], preferred_element_type=jnp.float32)
        return (right[:blocks] + right[blocks:2 * blocks]) + right[2 * blocks:]

    def waves(windows):
        data_coarse, data_fine = split(jnp.concatenate(windows, 1))
        both = jnp.dot(table_parts[...], data_coarse, preferred_element_type=jnp.float32)
        rest = jnp.dot(table_parts[:rows_out], data_fine, preferred_element_type=jnp.float32)
        result = both[:rows_out] + (both[rows_out:] + rest)
        return [result[:, i * wide:(i + 1) * wide] for i in range(len(windows))]

    def window_rows(block):
        return pl.ds(pl.multiple_of(block * half_len, half_len), NFFT)

    def transform(chunk, first, count):
        def spread(block, width):
            results = waves([held[chunk, window_rows(block + i), :] for i in range(width)])
            for i, result in enumerate(results):
                spectra[pl.ds(block + i, rows_out, stride=blocks), :] = result

        repeat(count // 2, 2, lambda step: spread(first + 2 * step, 2))
        if count % 2:
            spread(first + count - 1, 1)

    def half_transform(block):
        results = waves([half_held[side, window_rows(block), :] for side in range(2)])
        for side, result in enumerate(results):
            half_spectra[side, pl.ds(block, rows_out, stride=half_blocks), :] = result

    for side in range(2):
        half_keeping(side).wait()
        for peer in near:
            half_arriving(peer, side).wait_recv()
        halo_sending(my_snap, side, 0).wait_recv()
    repeat(half_blocks, 2, half_transform)
    spectra_keeping().start()

    for peer in near:
        for group in range(groups):
            spectra_sending(group, peer).start()
    pl.when(jnp.logical_not(at_cut))(lambda: send_far(0))

    def send_spectra(group):
        for peer in reversed(far):
            spectra_sending(group, peer).start()

    for group in range(min(AHEAD, groups)):
        send_spectra(group)

    def gram_product(data):
        data_coarse, data_fine = split(data)
        right = jnp.concatenate([data_coarse, data_fine], 0)
        both = lax.dot_general(data_coarse, right, (((1,), (1,)), ((), ())), preferred_element_type=jnp.float32)
        cross = both[:, 2 * blocks:]
        return both[:, :2 * blocks] + (cross + cross.T)

    def chunk_product(place):
        return gram_product(spectra[pl.ds(pl.multiple_of(place * 2 * blocks, 2 * blocks), 2 * blocks), :])

    def complex_gram(whole):
        top, turned = whole[:blocks], pltpu.roll(whole[blocks:], blocks, 1)
        lane = lax.broadcasted_iota(jnp.int32, top.shape, 1)
        return jnp.where(lane < blocks, top + turned, top - turned)

    def pair_up(first, second):
        first, second = complex_gram(first), complex_gram(second)
        row = lax.broadcasted_iota(jnp.int32, first.shape, 0)
        lane = lax.broadcasted_iota(jnp.int32, first.shape, 1)
        left = jnp.where(row >= lane, first, pltpu.roll(first, blocks, 1))
        right = jnp.where(row >= lane - blocks, pltpu.roll(second, blocks, 1), second)
        return jnp.where(lane < blocks, left, right)

    high_start = -(-half_rows // half_len)
    low_count = (half_rows - NFFT) // half_len + 1
    for chunk in range(last):
        keeping(chunk).wait()
        for peer in near:
            arriving(chunk, peer).wait_recv()
        transform(chunk, my_half * high_start, low_count)
        for peer in far:
            arriving(chunk, peer).wait_recv()
        if chunk == last - 1:
            for group in range(AHEAD, min(2 * AHEAD, groups)):
                send_spectra(group)
        transform(chunk, low_count, high_start - low_count)
        transform(chunk, (1 - my_half) * high_start, low_count)
        if chunk < last - 1:
            def accumulate(place, chunk=chunk):
                grams[place] = chunk_product(place) if chunk == 0 else grams[place] + chunk_product(place)

            repeat(kept_count, 4, accumulate)

    def early_gram(place):
        return grams[place] + chunk_product(place) if last > 1 else chunk_product(place)

    def early_pack(pair):
        packed[pl.ds(pl.multiple_of(pair * blocks, blocks), blocks)] = pair_up(early_gram(2 * pair), early_gram(2 * pair + 1))

    def early_share(owner, cell):
        return pl.ds(pl.multiple_of(owner * groups * blocks + cell * early_rows, 8), early_rows)

    def scattering(owner, step):
        return remote(packed.at[early_share(owner, cell_peer(step))], cell_slots.at[step - 1, owner],
                      cell_send.at[step - 1, owner], cell_recv.at[step - 1, owner], my_snap, cell_peer(step))

    def near_exchanging(peer):
        return remote(own_cells.at[peer], near_slots.at[lax.rem(my_snap, half_count)], near_send.at[peer],
                      near_recv.at[lax.rem(my_snap, half_count)], peer, my_cell)

    def near_exchanged(peer):
        return remote(own_cells.at[peer], near_slots.at[lax.rem(peer, half_count)], near_send.at[peer],
                      near_recv.at[lax.rem(peer, half_count)], peer, my_cell)

    def lending(source):
        place = lax.rem(source, half_count)
        return remote(own_cells.at[pl.ds(half_count - half_start, half_count)], lent_slots.at[place], lent_send.at[0],
                      lent_recv.at[place], outer, my_cell)

    def forwarding(peer):
        return remote(far_sums.at[lax.rem(peer, half_count)], far_slot, forward_send.at[peer], forward_recv.at[0], peer, my_cell)

    def gather_rows(cell):
        return pl.ds(pl.multiple_of(cell * early_rows, 8), early_rows)

    def gathering(step):
        return remote(own_part, gathered.at[gather_rows(my_cell)], gather_send.at[step - 1], gather_recv.at[my_cell], my_snap, cell_peer(step))

    def gather_arriving(step):
        return remote(own_part, gathered.at[gather_rows(cell_peer(step))], gather_send.at[step - 1], gather_recv.at[cell_peer(step)],
                      my_snap, cell_peer(step))

    for owner in range(snap_count):
        repeat(groups, 2, lambda pair, owner=owner: early_pack(owner * groups + pair))
        for step in range(1, cell_count):
            scattering(owner, step).start()

    def early_exchange():
        for owner in range(snap_count):
            total = packed[early_share(owner, my_cell)]
            for step in range(1, cell_count):
                scattering(owner, step).wait_recv()
                total = total + cell_slots[step - 1, owner]
            own_cells[owner] = total
        for peer in near:
            near_exchanging(peer).start()
        pl.when(jnp.logical_not(at_end))(lambda: lending(my_snap).start())

    def early_forward():
        @pl.when(at_end)
        def _():
            total = own_cells[pl.ds(half_count - half_start, half_count)]
            for peer in near:
                lending(peer).wait_recv()
                total = total + lent_slots[lax.rem(peer, half_count)]
            far_sums[...] = total
            for peer in far:
                forwarding(peer).start()

    def early_gather():
        part = own_cells[my_snap]
        for peer in near:
            near_exchanged(peer).wait_recv()
            part = part + near_slots[lax.rem(peer, half_count)]
        forwarding(my_snap).wait_recv()
        part = part + far_slot[...]
        own_part[...] = part
        for step in range(1, cell_count):
            gathering(step).start()
        gathered[gather_rows(my_cell)] = part

    def early_collect():
        for step in range(1, cell_count):
            gather_arriving(step).wait_recv()

    def late_gram(group, member):
        sets = []
        for place in range(half_count):
            for side in range(2):
                rows = [
                    landed[half * half_count + place, side, pl.ds(group * group_rows + (2 * member + part) * half_blocks, half_blocks), :]
                    for part in range(2)
                    for half in range(2)
                ]
                sets.append(jnp.concatenate(rows, 0))
        return gram_product(jnp.concatenate(sets, 1))

    def late_sending(group, step):
        return remote(late_slots.at[group, my_cell], late_slots.at[group, my_cell], late_send.at[group, step - 1],
                      late_recv.at[group, my_cell], my_snap, cell_peer(step))

    def late_arriving(group, step):
        return remote(late_slots.at[group, my_cell], late_slots.at[group, cell_peer(step)], late_send.at[group, step - 1],
                      late_recv.at[group, cell_peer(step)], my_snap, cell_peer(step))

    def late_share(group):
        for peer in others:
            spectra_arriving(group, peer).wait_recv()
        if 2 * AHEAD <= group + AHEAD < groups:
            send_spectra(group + AHEAD)
        late_slots[group, my_cell] = pair_up(late_gram(group, 0), late_gram(group, 1))
        for step in range(1, cell_count):
            late_sending(group, step).start()

    def late_sum(group):
        for step in range(1, cell_count):
            late_arriving(group, step).wait_recv()
        total = late_slots[group, 0]
        for cell in range(1, cell_count):
            total = total + late_slots[group, cell]
        total = (total + gathered[pl.ds(group * blocks, blocks)]) * scale
        tile = reorder(total)
        turned = tile.T
        rolled = pltpu.roll(tile, blocks, 1)
        before, after = sides[0, :blocks, :blocks], sides[1, :blocks, :blocks]
        for member in range(2):
            straight = (tile if member == 0 else rolled)[:, :blocks]
            mirrored = turned[member * blocks:(member + 1) * blocks]
            place = member * groups + group
            out_ref[place, 0] = jnp.where(before >= after, straight, mirrored)
            out_ref[place, 1] = jnp.where(before == after, 0.0, jnp.where(before >= after, -mirrored, straight))

    spectra_keeping().wait()
    def finish_late(done):
        for group in done:
            for peer in far:
                spectra_sending(group, peer).wait_send()
            for step in range(1, cell_count):
                late_sending(group, step).wait_send()

    def finish_early():
        for half in range(2):
            at_middle(half, lambda copy: copy.wait_send())
        for peer in near:
            for side in range(2):
                half_sending(peer, side).wait_send()
            for group in range(groups):
                spectra_sending(group, peer).wait_send()
        for chunk in range(last):
            for peer in others:
                sending(chunk, peer).wait_send()
        for step in range(1, cell_count):
            gathering(step).wait_send()
            for owner in range(snap_count):
                scattering(owner, step).wait_send()
        for peer in near:
            near_exchanging(peer).wait_send()
        pl.when(jnp.logical_not(at_end))(lambda: lending(my_snap).wait_send())

        @pl.when(at_end)
        def _():
            for peer in far:
                forwarding(peer).wait_send()

    ended = max(groups - 2, 0)
    ready = min(5, groups - 1)
    steps = {}
    for turn, step in ((0, early_exchange), (1, early_forward), (3, early_gather), (ready, early_collect)):
        steps.setdefault(min(turn, groups - 1), []).append(step)
    for group in range(groups):
        late_share(group)
        for step in steps.get(group, []):
            step()
        if group >= ready:
            for done in range(0 if group == ready else group - 1, group):
                late_sum(done)
        if group == max(groups - 2, 0):
            finish_late(range(ended))
        if group == max(groups - 2, ready):
            finish_early()
    late_sum(groups - 1)

    finish_late(range(ended, groups))


def pipelined_grams(pressure, block_starts, retained_bins, snap_count, cell_count, blocks):
    row_count, width_local = pressure.shape
    wide = LANES
    chunks = width_local // snap_count // wide
    kept_count = retained_bins.shape[0]
    groups = kept_count // snap_count // 2
    early_rows = groups * blocks // cell_count
    lanes = 2 * blocks
    half_len = NFFT // 2
    half_rows = snap_count // 2 * row_count
    halo = half_rows % half_len
    assert kept_count == blocks and cell_count & (cell_count - 1) == 0 and snap_count > 2
    assert halo == half_len // 2 and halo <= row_count and blocks % 2 == 0 and snap_count % 2 == 0
    whole_vmem = pl.BlockSpec(memory_space=pltpu.VMEM)
    scale = 1.0 / (width_local * cell_count)
    semaphores = pltpu.SemaphoreType.DMA
    return pl.pallas_call(
        functools.partial(pipeline_kernel, snap_count, cell_count, chunks, wide, kept_count, blocks, scale),
        out_shape=jax.ShapeDtypeStruct((2 * groups, 2, blocks, blocks), jnp.float32),
        in_specs=[pl.BlockSpec(memory_space=pl.ANY), whole_vmem],
        out_specs=whole_vmem,
        scratch_shapes=[
            pltpu.VMEM((chunks - 1, snap_count * row_count, wide), jnp.float32),
            pltpu.VMEM((2, half_rows + halo, wide), jnp.float32),
            pltpu.VMEM((2 * kept_count * blocks, wide), jnp.float32),
            pltpu.VMEM((2, kept_count * blocks, wide), jnp.float32),
            pltpu.VMEM((snap_count, 2, 2 * groups * blocks, wide), jnp.float32),
            pltpu.VMEM((kept_count, lanes, lanes), jnp.float32),
            pltpu.VMEM((NFFT // LANES, 2 * kept_count, LANES), jnp.float32),
            pltpu.VMEM((4 * kept_count, NFFT), jnp.bfloat16),
            pltpu.VMEM((2, lanes, lanes), jnp.bfloat16),
            pltpu.VMEM((2, lanes, lanes), jnp.float32),
            pltpu.VMEM((snap_count * groups * blocks, lanes), jnp.float32),
            pltpu.VMEM((cell_count - 1, snap_count, early_rows, lanes), jnp.float32),
            pltpu.VMEM((snap_count, early_rows, lanes), jnp.float32),
            pltpu.VMEM((snap_count // 2, early_rows, lanes), jnp.float32),
            pltpu.VMEM((snap_count // 2, snap_count // 2, early_rows, lanes), jnp.float32),
            pltpu.VMEM((snap_count // 2, early_rows, lanes), jnp.float32),
            pltpu.VMEM((early_rows, lanes), jnp.float32),
            pltpu.VMEM((early_rows, lanes), jnp.float32),
            pltpu.VMEM((groups * blocks, lanes), jnp.float32),
            pltpu.VMEM((groups, cell_count, blocks, lanes), jnp.float32),
            semaphores((chunks,)),
            semaphores((chunks, snap_count)),
            semaphores((chunks, snap_count)),
            semaphores((2,)),
            semaphores((snap_count, 2)),
            semaphores((snap_count, 2)),
            semaphores((snap_count, 2)),
            semaphores((2,)),
            semaphores((1,)),
            semaphores((groups, snap_count)),
            semaphores((groups, snap_count)),
            semaphores((cell_count - 1, snap_count)),
            semaphores((cell_count - 1, snap_count)),
            semaphores((snap_count,)),
            semaphores((snap_count // 2,)),
            semaphores((1,)),
            semaphores((snap_count // 2,)),
            semaphores((snap_count,)),
            semaphores((1,)),
            semaphores((cell_count - 1,)),
            semaphores((cell_count,)),
            semaphores((groups, cell_count - 1)),
            semaphores((groups, cell_count)),
            pltpu.SemaphoreType.REGULAR((snap_count - 2, 2)),
            pltpu.SemaphoreType.REGULAR((cell_count.bit_length() - 1,)),
        ],
        compiler_params=pltpu.CompilerParams(collective_id=2, has_side_effects=True, vmem_limit_bytes=46 * 2**20),
    )(pressure, jnp.stack([retained_bins, block_starts]))


def gather_kernel(snap_count, chunks, wide, kept_count, blocks, pressure_ref, bins_ref, out_ref, held, spectra, grams,
                  table_parts, own_sem, send_sem, recv_sem):
    my_snap, my_cell = lax.axis_index("snap"), lax.axis_index("cell")
    row_count = pressure_ref.shape[0]
    half_count = snap_count // 2
    my_half = my_snap // half_count
    half_len = NFFT // 2
    near = [my_half * half_count + lax.rem(my_snap + step, half_count) for step in range(1, half_count)]
    far = [(1 - my_half) * half_count + lax.rem(my_snap + step, half_count) for step in range(half_count)]

    barrier = pltpu.get_barrier_semaphore()
    for peer in near + far:
        pl.semaphore_signal(barrier, inc=1, device_id=(peer, my_cell), device_id_type=MESH)
    pl.semaphore_wait(barrier, snap_count - 1)

    def columns(chunk, owner):
        return pressure_ref.at[:, pl.ds(pl.multiple_of((chunk * snap_count + owner) * wide, wide), wide)]

    def landing(chunk, source):
        return held.at[chunk, pl.ds(pl.multiple_of(source * row_count, 8), row_count)]

    def sending(chunk, peer):
        return pltpu.make_async_remote_copy(
            src_ref=columns(chunk, peer),
            dst_ref=landing(chunk, my_snap),
            send_sem=send_sem.at[chunk, peer],
            recv_sem=recv_sem.at[chunk, my_snap],
            device_id=(peer, my_cell),
            device_id_type=MESH,
        )

    def arriving(chunk, peer):
        return pltpu.make_async_remote_copy(
            src_ref=columns(chunk, peer),
            dst_ref=landing(chunk, peer),
            send_sem=send_sem.at[chunk, peer],
            recv_sem=recv_sem.at[chunk, peer],
            device_id=(peer, my_cell),
            device_id_type=MESH,
        )

    def keeping(chunk):
        return pltpu.make_async_copy(columns(chunk, my_snap), landing(chunk, my_snap), own_sem.at[chunk])

    for chunk in range(chunks):
        for peer in near:
            sending(chunk, peer).start()
        keeping(chunk).start()
    for chunk in range(chunks):
        for peer in far:
            sending(chunk, peer).start()

    table = make_table(bins_ref[...]).T
    coarse = table.astype(jnp.bfloat16)
    rows_out = 2 * kept_count
    table_parts[:rows_out] = coarse
    table_parts[rows_out:] = (table - coarse.astype(jnp.float32)).astype(jnp.bfloat16)

    half_rows = snap_count * row_count // 2
    low_count = (half_rows - NFFT) // half_len + 1
    high_start = -(-half_rows // half_len)
    assert low_count == blocks - high_start

    def transform(chunk, first, count):
        def spread(block, width):
            data = jnp.concatenate(
                [held[chunk, pl.ds(pl.multiple_of((block + i) * half_len, half_len), NFFT), :] for i in range(width)], 1
            )
            data_coarse = data.astype(jnp.bfloat16)
            data_fine = (data - data_coarse.astype(jnp.float32)).astype(jnp.bfloat16)
            both = jnp.dot(table_parts[...], data_coarse, preferred_element_type=jnp.float32)
            rest = jnp.dot(table_parts[:rows_out], data_fine, preferred_element_type=jnp.float32)
            result = both[:rows_out] + (both[rows_out:] + rest)
            for i in range(width):
                spectra[pl.ds(block + i, rows_out, stride=blocks), :] = result[:, i * wide:(i + 1) * wide]

        repeat(count // 2, 2, lambda step: spread(first + 2 * step, 2))
        if count % 2:
            spread(first + count - 1, 1)

    def product(k):
        data = jnp.concatenate(
            [spectra[pl.ds(pl.multiple_of((k + part * kept_count) * blocks, blocks), blocks), :] for part in range(2)], 0
        )
        data_coarse = data.astype(jnp.bfloat16)
        data_fine = (data - data_coarse.astype(jnp.float32)).astype(jnp.bfloat16)
        right = jnp.concatenate([data_coarse, data_fine], 0)
        both = lax.dot_general(data_coarse, right, (((1,), (1,)), ((), ())), preferred_element_type=jnp.float32)
        cross = both[:, 2 * blocks:]
        return both[:, :2 * blocks] + (cross + cross.T)

    def complex_gram(k):
        whole = grams[k] + product(k) if chunks > 1 else product(k)
        top, turned = whole[:blocks], pltpu.roll(whole[blocks:], blocks, 1)
        lane = lax.broadcasted_iota(jnp.int32, top.shape, 1)
        return jnp.where(lane < blocks, top + turned, top - turned)

    for chunk in range(chunks):
        keeping(chunk).wait()
        for peer in near:
            arriving(chunk, peer).wait_recv()
        transform(chunk, my_half * high_start, low_count)
        for peer in far:
            arriving(chunk, peer).wait_recv()
        transform(chunk, low_count, high_start - low_count)
        transform(chunk, (1 - my_half) * high_start, low_count)
        if chunk < chunks - 1:
            def accumulate(k, chunk=chunk):
                grams[k] = product(k) if chunk == 0 else grams[k] + product(k)

            repeat(kept_count, 4, accumulate)

    pairs = kept_count // snap_count // 2

    def finish(place):
        k = place // pairs * (2 * pairs) + lax.rem(place, pairs)
        first, second = complex_gram(k), complex_gram(k + pairs)
        row = lax.broadcasted_iota(jnp.int32, first.shape, 0)
        lane = lax.broadcasted_iota(jnp.int32, first.shape, 1)
        left = jnp.where(row >= lane, first, pltpu.roll(first, blocks, 1))
        right = jnp.where(row >= lane - blocks, pltpu.roll(second, blocks, 1), second)
        return jnp.where(lane < blocks, left, right)

    def write(place):
        out_ref[place] = finish(place)

    repeat(kept_count // 2, 2, write)
    for chunk in range(chunks):
        for peer in near + far:
            sending(chunk, peer).wait_send()


def local_grams(pressure, retained_bins, snap_count, blocks):
    row_count, width_local = pressure.shape
    wide = LANES
    chunks = width_local // snap_count // wide
    kept_count = retained_bins.shape[0]
    whole_vmem = pl.BlockSpec(memory_space=pltpu.VMEM)
    return pl.pallas_call(
        functools.partial(gather_kernel, snap_count, chunks, wide, kept_count, blocks),
        out_shape=jax.ShapeDtypeStruct((kept_count // 2, blocks, 2 * blocks), jnp.float32),
        in_specs=[pl.BlockSpec(memory_space=pl.ANY), whole_vmem],
        out_specs=whole_vmem,
        scratch_shapes=[
            pltpu.VMEM((chunks, snap_count * row_count, wide), jnp.float32),
            pltpu.VMEM((2 * kept_count * blocks, wide), jnp.float32),
            pltpu.VMEM((kept_count, 2 * blocks, 2 * blocks), jnp.float32),
            pltpu.VMEM((4 * kept_count, NFFT), jnp.bfloat16),
            pltpu.SemaphoreType.DMA((chunks,)),
            pltpu.SemaphoreType.DMA((chunks, snap_count)),
            pltpu.SemaphoreType.DMA((chunks, snap_count)),
        ],
        compiler_params=pltpu.CompilerParams(collective_id=1, has_side_effects=True),
    )(pressure, retained_bins.reshape(1, kept_count))


def reduce_kernel(snap_count, cell_count, scale, gram_ref, out_ref, cell_slots, own_cells, snap_slots, own_part, gathered,
                  cell_send, cell_recv, snap_send, snap_recv, gather_send, gather_recv):
    my_snap, my_cell = lax.axis_index("snap"), lax.axis_index("cell")

    def cell_peer(step):
        return lax.rem(my_cell + step, cell_count)

    def snap_peer(step):
        return lax.rem(my_snap + step, snap_count)

    barrier = pltpu.get_barrier_semaphore()
    for step in range(1, cell_count):
        pl.semaphore_signal(barrier, inc=1, device_id=(my_snap, cell_peer(step)), device_id_type=MESH)
    for step in range(1, snap_count):
        pl.semaphore_signal(barrier, inc=1, device_id=(snap_peer(step), my_cell), device_id_type=MESH)
    pl.semaphore_wait(barrier, cell_count + snap_count - 2)

    scatters = [
        pltpu.make_async_remote_copy(
            src_ref=gram_ref.at[:, cell_peer(step)],
            dst_ref=cell_slots.at[step - 1],
            send_sem=cell_send.at[step - 1],
            recv_sem=cell_recv.at[step - 1],
            device_id=(my_snap, cell_peer(step)),
            device_id_type=MESH,
        )
        for step in range(1, cell_count)
    ]
    for copy in scatters:
        copy.start()
    total = gram_ref[:, my_cell]
    for step in range(1, cell_count):
        scatters[step - 1].wait_recv()
        total = total + cell_slots[step - 1]
    own_cells[...] = total

    exchanges = [
        pltpu.make_async_remote_copy(
            src_ref=own_cells.at[snap_peer(step)],
            dst_ref=snap_slots.at[step - 1],
            send_sem=snap_send.at[step - 1],
            recv_sem=snap_recv.at[step - 1],
            device_id=(snap_peer(step), my_cell),
            device_id_type=MESH,
        )
        for step in range(1, snap_count)
    ]
    for copy in exchanges:
        copy.start()
    part = own_cells[my_snap]
    for step in range(1, snap_count):
        exchanges[step - 1].wait_recv()
        part = part + snap_slots[step - 1]
    own_part[...] = part * scale

    gathers = [
        pltpu.make_async_remote_copy(
            src_ref=own_part,
            dst_ref=gathered.at[my_cell],
            send_sem=gather_send.at[step - 1],
            recv_sem=gather_recv.at[step - 1],
            device_id=(my_snap, cell_peer(step)),
            device_id_type=MESH,
        )
        for step in range(1, cell_count)
    ]
    for copy in gathers:
        copy.start()
    out_ref[my_cell] = own_part[...]
    for step in range(1, cell_count):
        gathers[step - 1].wait_recv()
        source = lax.rem(my_cell + cell_count - step, cell_count)
        out_ref[source] = gathered[source]
    for copy in scatters + exchanges + gathers:
        copy.wait_send()


def reduce_grams(packed, scale):
    snap_count, cell_count, rows, lanes = packed.shape
    whole_vmem = pl.BlockSpec(memory_space=pltpu.VMEM)
    return pl.pallas_call(
        functools.partial(reduce_kernel, snap_count, cell_count, scale),
        out_shape=jax.ShapeDtypeStruct((cell_count, rows, lanes), jnp.float32),
        in_specs=[whole_vmem],
        out_specs=whole_vmem,
        scratch_shapes=[
            pltpu.VMEM((cell_count - 1, snap_count, rows, lanes), jnp.float32),
            pltpu.VMEM((snap_count, rows, lanes), jnp.float32),
            pltpu.VMEM((snap_count - 1, rows, lanes), jnp.float32),
            pltpu.VMEM((rows, lanes), jnp.float32),
            pltpu.VMEM((cell_count, rows, lanes), jnp.float32),
            pltpu.SemaphoreType.DMA((cell_count - 1,)),
            pltpu.SemaphoreType.DMA((cell_count - 1,)),
            pltpu.SemaphoreType.DMA((snap_count - 1,)),
            pltpu.SemaphoreType.DMA((snap_count - 1,)),
            pltpu.SemaphoreType.DMA((cell_count - 1,)),
            pltpu.SemaphoreType.DMA((cell_count - 1,)),
        ],
        compiler_params=pltpu.CompilerParams(collective_id=0, has_side_effects=True),
    )(packed)


def on_device(pressure, block_starts, retained_bins):
    snap_count = lax.axis_size("snap")
    row_count, width_local = pressure.shape
    kept_count = retained_bins.shape[0]
    blocks = block_starts.shape[0]
    lower = jnp.arange(blocks)[:, None] >= jnp.arange(blocks)[None, :]
    cell_count = lax.axis_size("cell")
    pairs = kept_count // snap_count // 2
    if pairs * blocks % (8 * cell_count) == 0 and width_local // snap_count // LANES > 1:
        return pipelined_grams(pressure, block_starts, retained_bins, snap_count, cell_count, blocks)
    halves = local_grams(pressure, retained_bins, snap_count, blocks)
    packed = halves.reshape(snap_count, cell_count, pairs * blocks // cell_count, 2 * blocks)
    reduced = reduce_grams(packed, 1.0 / (width_local * cell_count))
    paired = reduced.reshape(pairs, blocks, 2 * blocks)
    joined = jnp.concatenate([paired[:, :, :blocks], paired[:, :, blocks:]], 0)
    mirrored = joined.transpose(0, 2, 1)
    diagonal = jnp.eye(blocks, dtype=bool)
    own_real = jnp.where(lower, joined, mirrored)
    own_imag = jnp.where(diagonal, 0.0, jnp.where(lower, -mirrored, joined))
    own_block = jnp.stack([own_real, own_imag], 1)
    order = (block_starts[:, None] // (NFFT // 2) == jnp.arange(blocks)[None, :]).astype(jnp.float32)
    turned = jnp.einsum("kpij,dj->kpid", own_block, order, precision=lax.Precision.HIGHEST)
    return jnp.einsum("bi,kpid->kpbd", order, turned, precision=lax.Precision.HIGHEST)


def solution(mesh):
    placed = (P("snap", "cell"), P(), P())
    return jax.shard_map(
        on_device,
        mesh=mesh,
        in_specs=placed,
        out_specs=P("snap", None, None, None),
        check_vma=False,
    )
```

```python
import functools

import jax
import jax.numpy as jnp
from jax import lax
from jax.experimental import pallas as pl
from jax.experimental.pallas import tpu as pltpu
from jax.sharding import PartitionSpec as P

NFFT = 256
LANES = 128
AHEAD = 3
MESH = pl.DeviceIdType.MESH


def make_table(bins):
    offsets = lax.broadcasted_iota(jnp.int32, (NFFT, bins.shape[1]), 0)
    window = 0.5 - 0.5 * jnp.cos(2.0 * jnp.pi * offsets.astype(jnp.float32) / NFFT)
    norm_factor = 1.0 / jnp.sqrt(jnp.sum(window * window, axis=0, keepdims=True))
    phase_steps = (bins * offsets) & (NFFT - 1)
    angles = 2.0 * jnp.pi * phase_steps.astype(jnp.float32) / NFFT
    return jnp.concatenate([window * norm_factor * jnp.cos(angles), -window * norm_factor * jnp.sin(angles)], 1)


def repeat(count, unroll, step):
    def body(turn, carry):
        for extra in range(unroll):
            step(turn * unroll + extra)
        return carry

    lax.fori_loop(0, count // unroll, body, 0)
    for rest in range(count // unroll * unroll, count):
        step(rest)


def pipeline_kernel(snap_count, cell_count, chunks, wide, kept_count, blocks, scale, pressure_ref, index_ref, out_ref, held, half_held,
                    spectra, half_spectra, landed, grams, table_rows, table_parts, turns, sides, packed, cell_slots, own_cells, near_slots, lent_slots, far_sums, far_slot, own_part,
                    gathered, late_slots, own_sem, send_sem, recv_sem, half_own, half_send, half_recv, halo_send, halo_recv, keep_sem,
                    spec_send, spec_recv, cell_send, cell_recv, near_send, near_recv, lent_send, lent_recv, forward_send, forward_recv,
                    gather_send, gather_recv, late_send, late_recv, line_sem, flip_sem):
    my_snap, my_cell = lax.axis_index("snap"), lax.axis_index("cell")
    row_count = pressure_ref.shape[0]
    half_count = snap_count // 2
    my_half = my_snap // half_count
    half_start = my_half * half_count
    half_len = NFFT // 2
    half_rows = half_count * row_count
    half_blocks = blocks // 2
    halo = half_rows % half_len
    last = chunks - 1
    rows_out = 2 * kept_count
    groups = kept_count // snap_count // 2
    group_rows = 4 * half_blocks
    early_rows = groups * blocks // cell_count
    near = [half_start + lax.rem(my_snap + step, half_count) for step in range(1, half_count)]
    far = [half_count - my_half + step * (1 - 2 * my_half) for step in range(half_count)]
    others = near + far
    outer = my_half * (snap_count - 1)
    at_end = my_snap == outer

    def cell_peer(step):
        return lax.rem(my_cell + step, cell_count)

    bits = cell_count.bit_length() - 1

    def cell_flip(bit):
        return my_cell + 2 ** bit * (1 - 2 * lax.rem(my_cell // 2 ** bit, 2))

    def along(step):
        pl.when(my_snap > 0)(lambda: step(my_snap - 1, 1))
        pl.when(my_snap < snap_count - 1)(lambda: step(my_snap + 1, 0))

    barrier = pltpu.get_barrier_semaphore()
    along(lambda snap, side: pl.semaphore_signal(barrier, inc=1, device_id=(snap, my_cell), device_id_type=MESH))
    for bit in range(bits):
        pl.semaphore_signal(barrier, inc=1, device_id=(my_snap, cell_flip(bit)), device_id_type=MESH)
    pl.semaphore_wait(barrier, bits + jnp.minimum(my_snap, 1) + jnp.minimum(snap_count - 1 - my_snap, 1))

    def remote(source, target, send, recv, snap, cell):
        return pltpu.make_async_remote_copy(
            src_ref=source, dst_ref=target, send_sem=send, recv_sem=recv, device_id=(snap, cell), device_id_type=MESH
        )

    def columns(chunk, owner):
        return pl.ds(pl.multiple_of((chunk * snap_count + owner) * wide, wide), wide)

    def rows_of(source):
        return pl.ds(pl.multiple_of(source * row_count, 8), row_count)

    def sending(chunk, peer):
        return remote(pressure_ref.at[:, columns(chunk, peer)], held.at[chunk, rows_of(my_snap)],
                      send_sem.at[chunk, peer], recv_sem.at[chunk, my_snap], peer, my_cell)

    def arriving(chunk, peer):
        return remote(pressure_ref.at[:, columns(chunk, peer)], held.at[chunk, rows_of(peer)],
                      send_sem.at[chunk, peer], recv_sem.at[chunk, peer], peer, my_cell)

    def keeping(chunk):
        return pltpu.make_async_copy(pressure_ref.at[:, columns(chunk, my_snap)], held.at[chunk, rows_of(my_snap)], own_sem.at[chunk])

    def half_columns(peer, side):
        return columns(last, lax.rem(peer, half_count) + side * half_count)

    def half_place(source):
        return pl.ds(pl.multiple_of(my_half * halo + lax.rem(source, half_count) * row_count, 8), row_count)

    def half_sending(peer, side):
        return remote(pressure_ref.at[:, half_columns(peer, side)], half_held.at[side, half_place(my_snap)],
                      half_send.at[peer, side], half_recv.at[my_snap, side], peer, my_cell)

    def half_arriving(peer, side):
        return remote(pressure_ref.at[:, half_columns(my_snap, side)], half_held.at[side, half_place(peer)],
                      half_send.at[peer, side], half_recv.at[peer, side], peer, my_cell)

    def half_keeping(side):
        return pltpu.make_async_copy(pressure_ref.at[:, half_columns(my_snap, side)], half_held.at[side, half_place(my_snap)],
                                     half_own.at[side])

    def halo_sending(peer, side, half):
        first, place = (row_count - halo, 0) if half == 0 else (0, half_rows)
        return remote(pressure_ref.at[pl.ds(first, halo), half_columns(peer, side)], half_held.at[side, pl.ds(place, halo)],
                      halo_send.at[peer, side], halo_recv.at[side], peer, my_cell)

    def spectra_rows(owner, group):
        return pl.ds(pl.multiple_of((owner * groups + group) * group_rows, group_rows), group_rows)

    def spectra_sending(group, peer):
        return remote(half_spectra.at[:, spectra_rows(peer, group)], landed.at[my_snap, :, pl.ds(group * group_rows, group_rows)],
                      spec_send.at[group, peer], spec_recv.at[group, my_snap], peer, my_cell)

    def spectra_arriving(group, peer):
        return remote(half_spectra.at[:, spectra_rows(peer, group)], landed.at[peer, :, pl.ds(group * group_rows, group_rows)],
                      spec_send.at[group, peer], spec_recv.at[group, peer], peer, my_cell)

    def spectra_keeping():
        own = pl.ds(pl.multiple_of(my_snap * groups * group_rows, group_rows), groups * group_rows)
        return pltpu.make_async_copy(half_spectra.at[:, own], landed.at[my_snap], keep_sem.at[0])

    def at_middle(half, step):
        @pl.when(my_snap == half_count - 1 + half)
        def _():
            for peer in far:
                for side in range(2):
                    step(halo_sending(peer, side, half))

    at_cut = my_snap == half_count - 1 + my_half

    @pl.when(at_cut)
    def _():
        sending(0, far[0]).start()

    for turn in range(snap_count - 2):
        along(lambda snap, side, turn=turn: pl.semaphore_signal(
            line_sem.at[turn, side], inc=1, device_id=(snap, my_cell), device_id_type=MESH))
        along(lambda snap, side, turn=turn: pl.semaphore_wait(line_sem.at[turn, 1 - side], 1))
    for bit in range(bits):
        pl.semaphore_signal(flip_sem.at[bit], inc=1, device_id=(my_snap, cell_flip(bit)), device_id_type=MESH)
        pl.semaphore_wait(flip_sem.at[bit], 1)

    for half in range(2):
        at_middle(half, lambda copy: copy.start())
    for side in range(2):
        for peer in near:
            half_sending(peer, side).start()
        half_keeping(side).start()
    for chunk in range(last):
        for peer in near:
            sending(chunk, peer).start()
        keeping(chunk).start()
    def send_far(begun):
        for chunk in range(last):
            for peer in far[begun if chunk == 0 else 0:]:
                sending(chunk, peer).start()

    pl.when(at_cut)(lambda: send_far(1))

    table = make_table(index_ref[:1, :kept_count]).T
    for side in range(NFFT // LANES):
        for part in range(2):
            for slot in range(2 * snap_count):
                first = part * kept_count + slot * groups
                place = slot // 2 * 4 * groups + slot % 2 * 2 + part
                table_rows[side, pl.ds(place, groups, stride=4), :] = table[first:first + groups, side * LANES:(side + 1) * LANES]
    table = jnp.concatenate([table_rows[side] for side in range(NFFT // LANES)], 1)
    coarse = table.astype(jnp.bfloat16)
    table_parts[:rows_out] = coarse
    table_parts[rows_out:] = (table - coarse.astype(jnp.float32)).astype(jnp.bfloat16)

    lanes = 2 * blocks
    starts = jnp.concatenate([index_ref[1:, :blocks]] * 2, 1).astype(jnp.float32)
    across = jnp.broadcast_to(starts, (lanes, lanes))
    down = across.T
    sides[0] = down
    sides[1] = across
    row = lax.broadcasted_iota(jnp.int32, (lanes, lanes), 0)
    lane = lax.broadcasted_iota(jnp.int32, (lanes, lanes), 1)
    same_side = (row < blocks) == (lane < blocks)
    row_slot = (half_len * jnp.where(row < blocks, row, row - blocks)).astype(jnp.float32)
    lane_slot = (half_len * jnp.where(lane < blocks, lane, lane - blocks)).astype(jnp.float32)
    turns[0] = jnp.where(same_side & (down == lane_slot), 1.0, 0.0).astype(jnp.bfloat16)
    turns[1] = jnp.where(same_side & (across == row_slot), 1.0, 0.0).astype(jnp.bfloat16)

    def split(data):
        coarse = data.astype(jnp.bfloat16)
        return coarse, (data - coarse.astype(jnp.float32)).astype(jnp.bfloat16)

    def thirds(data):
        coarse, rest = split(data)
        middle = data - coarse.astype(jnp.float32)
        return [coarse, rest, (middle - rest.astype(jnp.float32)).astype(jnp.bfloat16)]

    def reorder(tile):
        left = jnp.dot(turns[0, :blocks, :blocks], jnp.concatenate(thirds(tile), 1), preferred_element_type=jnp.float32)
        tile = (left[:, :lanes] + left[:, lanes:2 * lanes]) + left[:, 2 * lanes:]
        right = jnp.dot(jnp.concatenate(thirds(tile), 0), turns[1], preferred_element_type=jnp.float32)
        return (right[:blocks] + right[blocks:2 * blocks]) + right[2 * blocks:]

    def waves(windows):
        data_coarse, data_fine = split(jnp.concatenate(windows, 1))
        both = jnp.dot(table_parts[...], data_coarse, preferred_element_type=jnp.float32)
        rest = jnp.dot(table_parts[:rows_out], data_fine, preferred_element_type=jnp.float32)
        result = both[:rows_out] + (both[rows_out:] + rest)
        return [result[:, i * wide:(i + 1) * wide] for i in range(len(windows))]

    def window_rows(block):
        return pl.ds(pl.multiple_of(block * half_len, half_len), NFFT)

    def transform(chunk, first, count):
        def spread(block, width):
            results = waves([held[chunk, window_rows(block + i), :] for i in range(width)])
            for i, result in enumerate(results):
                spectra[pl.ds(block + i, rows_out, stride=blocks), :] = result

        repeat(count // 2, 2, lambda step: spread(first + 2 * step, 2))
        if count % 2:
            spread(first + count - 1, 1)

    def half_transform(block):
        results = waves([half_held[side, window_rows(block), :] for side in range(2)])
        for side, result in enumerate(results):
            half_spectra[side, pl.ds(block, rows_out, stride=half_blocks), :] = result

    for side in range(2):
        half_keeping(side).wait()
        for peer in near:
            half_arriving(peer, side).wait_recv()
        halo_sending(my_snap, side, 0).wait_recv()
    repeat(half_blocks, 2, half_transform)
    spectra_keeping().start()

    for peer in near:
        for group in range(groups):
            spectra_sending(group, peer).start()
    pl.when(jnp.logical_not(at_cut))(lambda: send_far(0))

    def send_spectra(group):
        for peer in reversed(far):
            spectra_sending(group, peer).start()

    for group in range(min(AHEAD, groups)):
        send_spectra(group)

    def raw_product(data):
        data_coarse, data_fine = split(data)
        right = jnp.concatenate([data_coarse, data_fine], 0)
        return lax.dot_general(data_coarse, right, (((1,), (1,)), ((), ())), preferred_element_type=jnp.float32)

    def gram_product(data):
        return symmetric(raw_product(data))

    def symmetric(both):
        cross = both[:, 2 * blocks:]
        return both[:, :2 * blocks] + (cross + cross.T)

    def chunk_product(place):
        return gram_product(spectra[pl.ds(pl.multiple_of(place * 2 * blocks, 2 * blocks), 2 * blocks), :])

    def complex_gram(whole):
        top, turned = whole[:blocks], pltpu.roll(whole[blocks:], blocks, 1)
        lane = lax.broadcasted_iota(jnp.int32, top.shape, 1)
        return jnp.where(lane < blocks, top + turned, top - turned)

    def pair_up(first, second):
        first, second = complex_gram(first), complex_gram(second)
        row = lax.broadcasted_iota(jnp.int32, first.shape, 0)
        lane = lax.broadcasted_iota(jnp.int32, first.shape, 1)
        left = jnp.where(row >= lane, first, pltpu.roll(first, blocks, 1))
        right = jnp.where(row >= lane - blocks, pltpu.roll(second, blocks, 1), second)
        return jnp.where(lane < blocks, left, right)

    high_start = -(-half_rows // half_len)
    low_count = (half_rows - NFFT) // half_len + 1
    for chunk in range(last):
        keeping(chunk).wait()
        for peer in near:
            arriving(chunk, peer).wait_recv()
        transform(chunk, my_half * high_start, low_count)
        for peer in far:
            arriving(chunk, peer).wait_recv()
        if chunk == last - 1:
            for group in range(AHEAD, min(2 * AHEAD, groups)):
                send_spectra(group)
        transform(chunk, low_count, high_start - low_count)
        transform(chunk, (1 - my_half) * high_start, low_count)
        if chunk < last - 1:
            def accumulate(place, chunk=chunk):
                grams[place] = chunk_product(place) if chunk == 0 else grams[place] + chunk_product(place)

            repeat(kept_count, 4, accumulate)

    def early_gram(place):
        return grams[place] + chunk_product(place) if last > 1 else chunk_product(place)

    def early_pack(pair):
        packed[pl.ds(pl.multiple_of(pair * blocks, blocks), blocks)] = pair_up(early_gram(2 * pair), early_gram(2 * pair + 1))

    def early_share(owner, cell):
        return pl.ds(pl.multiple_of(owner * groups * blocks + cell * early_rows, 8), early_rows)

    def scattering(owner, step):
        return remote(packed.at[early_share(owner, cell_peer(step))], cell_slots.at[step - 1, owner],
                      cell_send.at[step - 1, owner], cell_recv.at[step - 1, owner], my_snap, cell_peer(step))

    def near_exchanging(peer):
        return remote(own_cells.at[peer], near_slots.at[lax.rem(my_snap, half_count)], near_send.at[peer],
                      near_recv.at[lax.rem(my_snap, half_count)], peer, my_cell)

    def near_exchanged(peer):
        return remote(own_cells.at[peer], near_slots.at[lax.rem(peer, half_count)], near_send.at[peer],
                      near_recv.at[lax.rem(peer, half_count)], peer, my_cell)

    def lending(source):
        place = lax.rem(source, half_count)
        return remote(own_cells.at[pl.ds(half_count - half_start, half_count)], lent_slots.at[place], lent_send.at[0],
                      lent_recv.at[place], outer, my_cell)

    def forwarding(peer):
        return remote(far_sums.at[lax.rem(peer, half_count)], far_slot, forward_send.at[peer], forward_recv.at[0], peer, my_cell)

    def gather_rows(cell):
        return pl.ds(pl.multiple_of(cell * early_rows, 8), early_rows)

    def gathering(step):
        return remote(own_part, gathered.at[gather_rows(my_cell)], gather_send.at[step - 1], gather_recv.at[my_cell], my_snap, cell_peer(step))

    def gather_arriving(step):
        return remote(own_part, gathered.at[gather_rows(cell_peer(step))], gather_send.at[step - 1], gather_recv.at[cell_peer(step)],
                      my_snap, cell_peer(step))

    for owner in range(snap_count):
        repeat(groups, 2, lambda pair, owner=owner: early_pack(owner * groups + pair))
        for step in range(1, cell_count):
            scattering(owner, step).start()

    def early_exchange():
        for owner in range(snap_count):
            total = packed[early_share(owner, my_cell)]
            for step in range(1, cell_count):
                scattering(owner, step).wait_recv()
                total = total + cell_slots[step - 1, owner]
            own_cells[owner] = total
        for peer in near:
            near_exchanging(peer).start()
        pl.when(jnp.logical_not(at_end))(lambda: lending(my_snap).start())

    def early_forward():
        @pl.when(at_end)
        def _():
            total = own_cells[pl.ds(half_count - half_start, half_count)]
            for peer in near:
                lending(peer).wait_recv()
                total = total + lent_slots[lax.rem(peer, half_count)]
            far_sums[...] = total
            for peer in far:
                forwarding(peer).start()

    def early_gather():
        part = own_cells[my_snap]
        for peer in near:
            near_exchanged(peer).wait_recv()
            part = part + near_slots[lax.rem(peer, half_count)]
        forwarding(my_snap).wait_recv()
        part = part + far_slot[...]
        own_part[...] = part
        for step in range(1, cell_count):
            gathering(step).start()
        gathered[gather_rows(my_cell)] = part

    def early_collect():
        for step in range(1, cell_count):
            gather_arriving(step).wait_recv()

    def late_product(group, member, place):
        sides = []
        for side in range(2):
            rows = [
                landed[half * half_count + place, side, pl.ds(group * group_rows + (2 * member + part) * half_blocks, half_blocks), :]
                for part in range(2)
                for half in range(2)
            ]
            sides.append(jnp.concatenate(rows, 0))
        return raw_product(jnp.concatenate(sides, 1))

    def late_sending(group, step):
        return remote(late_slots.at[group, my_cell], late_slots.at[group, my_cell], late_send.at[group, step - 1],
                      late_recv.at[group, my_cell], my_snap, cell_peer(step))

    def late_arriving(group, step):
        return remote(late_slots.at[group, my_cell], late_slots.at[group, cell_peer(step)], late_send.at[group, step - 1],
                      late_recv.at[group, cell_peer(step)], my_snap, cell_peer(step))

    def late_share(group):
        for peer in near:
            spectra_arriving(group, peer).wait_recv()
        grams_here = [0.0, 0.0]
        for peer in reversed(far):
            spectra_arriving(group, peer).wait_recv()
            for member in range(2):
                grams_here[member] += late_product(group, member, lax.rem(peer, half_count))
        if 2 * AHEAD <= group + AHEAD < groups:
            send_spectra(group + AHEAD)
        late_slots[group, my_cell] = pair_up(symmetric(grams_here[0]), symmetric(grams_here[1]))
        for step in range(1, cell_count):
            late_sending(group, step).start()

    def late_sum(group):
        for step in range(1, cell_count):
            late_arriving(group, step).wait_recv()
        total = late_slots[group, 0]
        for cell in range(1, cell_count):
            total = total + late_slots[group, cell]
        total = (total + gathered[pl.ds(group * blocks, blocks)]) * scale
        tile = reorder(total)
        turned = tile.T
        rolled = pltpu.roll(tile, blocks, 1)
        before, after = sides[0, :blocks, :blocks], sides[1, :blocks, :blocks]
        for member in range(2):
            straight = (tile if member == 0 else rolled)[:, :blocks]
            mirrored = turned[member * blocks:(member + 1) * blocks]
            place = member * groups + group
            out_ref[place, 0] = jnp.where(before >= after, straight, mirrored)
            out_ref[place, 1] = jnp.where(before == after, 0.0, jnp.where(before >= after, -mirrored, straight))

    spectra_keeping().wait()
    def finish_late(done):
        for group in done:
            for peer in far:
                spectra_sending(group, peer).wait_send()
            for step in range(1, cell_count):
                late_sending(group, step).wait_send()

    def finish_early():
        for half in range(2):
            at_middle(half, lambda copy: copy.wait_send())
        for peer in near:
            for side in range(2):
                half_sending(peer, side).wait_send()
            for group in range(groups):
                spectra_sending(group, peer).wait_send()
        for chunk in range(last):
            for peer in others:
                sending(chunk, peer).wait_send()
        for step in range(1, cell_count):
            gathering(step).wait_send()
            for owner in range(snap_count):
                scattering(owner, step).wait_send()
        for peer in near:
            near_exchanging(peer).wait_send()
        pl.when(jnp.logical_not(at_end))(lambda: lending(my_snap).wait_send())

        @pl.when(at_end)
        def _():
            for peer in far:
                forwarding(peer).wait_send()

    ended = max(groups - 2, 0)
    ready = min(5, groups - 1)
    steps = {}
    for turn, step in ((0, early_exchange), (1, early_forward), (3, early_gather), (ready, early_collect)):
        steps.setdefault(min(turn, groups - 1), []).append(step)
    for group in range(groups):
        late_share(group)
        for step in steps.get(group, []):
            step()
        if group >= ready:
            for done in range(0 if group == ready else group - 1, group):
                late_sum(done)
        if group == max(groups - 2, 0):
            finish_late(range(ended))
        if group == max(groups - 2, ready):
            finish_early()
    finish_late(range(ended, groups - 1))
    late_sum(groups - 1)
    finish_late([groups - 1])


def pipelined_grams(pressure, block_starts, retained_bins, snap_count, cell_count, blocks):
    row_count, width_local = pressure.shape
    wide = LANES
    chunks = width_local // snap_count // wide
    kept_count = retained_bins.shape[0]
    groups = kept_count // snap_count // 2
    early_rows = groups * blocks // cell_count
    lanes = 2 * blocks
    half_len = NFFT // 2
    half_rows = snap_count // 2 * row_count
    halo = half_rows % half_len
    assert kept_count == blocks and cell_count & (cell_count - 1) == 0 and snap_count > 2
    assert halo == half_len // 2 and halo <= row_count and blocks % 2 == 0 and snap_count % 2 == 0
    whole_vmem = pl.BlockSpec(memory_space=pltpu.VMEM)
    scale = 1.0 / (width_local * cell_count)
    semaphores = pltpu.SemaphoreType.DMA
    return pl.pallas_call(
        functools.partial(pipeline_kernel, snap_count, cell_count, chunks, wide, kept_count, blocks, scale),
        out_shape=jax.ShapeDtypeStruct((2 * groups, 2, blocks, blocks), jnp.float32),
        in_specs=[pl.BlockSpec(memory_space=pl.ANY), whole_vmem],
        out_specs=whole_vmem,
        scratch_shapes=[
            pltpu.VMEM((chunks - 1, snap_count * row_count, wide), jnp.float32),
            pltpu.VMEM((2, half_rows + halo, wide), jnp.float32),
            pltpu.VMEM((2 * kept_count * blocks, wide), jnp.float32),
            pltpu.VMEM((2, kept_count * blocks, wide), jnp.float32),
            pltpu.VMEM((snap_count, 2, 2 * groups * blocks, wide), jnp.float32),
            pltpu.VMEM((kept_count, lanes, lanes), jnp.float32),
            pltpu.VMEM((NFFT // LANES, 2 * kept_count, LANES), jnp.float32),
            pltpu.VMEM((4 * kept_count, NFFT), jnp.bfloat16),
            pltpu.VMEM((2, lanes, lanes), jnp.bfloat16),
            pltpu.VMEM((2, lanes, lanes), jnp.float32),
            pltpu.VMEM((snap_count * groups * blocks, lanes), jnp.float32),
            pltpu.VMEM((cell_count - 1, snap_count, early_rows, lanes), jnp.float32),
            pltpu.VMEM((snap_count, early_rows, lanes), jnp.float32),
            pltpu.VMEM((snap_count // 2, early_rows, lanes), jnp.float32),
            pltpu.VMEM((snap_count // 2, snap_count // 2, early_rows, lanes), jnp.float32),
            pltpu.VMEM((snap_count // 2, early_rows, lanes), jnp.float32),
            pltpu.VMEM((early_rows, lanes), jnp.float32),
            pltpu.VMEM((early_rows, lanes), jnp.float32),
            pltpu.VMEM((groups * blocks, lanes), jnp.float32),
            pltpu.VMEM((groups, cell_count, blocks, lanes), jnp.float32),
            semaphores((chunks,)),
            semaphores((chunks, snap_count)),
            semaphores((chunks, snap_count)),
            semaphores((2,)),
            semaphores((snap_count, 2)),
            semaphores((snap_count, 2)),
            semaphores((snap_count, 2)),
            semaphores((2,)),
            semaphores((1,)),
            semaphores((groups, snap_count)),
            semaphores((groups, snap_count)),
            semaphores((cell_count - 1, snap_count)),
            semaphores((cell_count - 1, snap_count)),
            semaphores((snap_count,)),
            semaphores((snap_count // 2,)),
            semaphores((1,)),
            semaphores((snap_count // 2,)),
            semaphores((snap_count,)),
            semaphores((1,)),
            semaphores((cell_count - 1,)),
            semaphores((cell_count,)),
            semaphores((groups, cell_count - 1)),
            semaphores((groups, cell_count)),
            pltpu.SemaphoreType.REGULAR((snap_count - 2, 2)),
            pltpu.SemaphoreType.REGULAR((cell_count.bit_length() - 1,)),
        ],
        compiler_params=pltpu.CompilerParams(collective_id=2, has_side_effects=True, vmem_limit_bytes=46 * 2**20),
    )(pressure, jnp.stack([retained_bins, block_starts]))


def gather_kernel(snap_count, chunks, wide, kept_count, blocks, pressure_ref, bins_ref, out_ref, held, spectra, grams,
                  table_parts, own_sem, send_sem, recv_sem):
    my_snap, my_cell = lax.axis_index("snap"), lax.axis_index("cell")
    row_count = pressure_ref.shape[0]
    half_count = snap_count // 2
    my_half = my_snap // half_count
    half_len = NFFT // 2
    near = [my_half * half_count + lax.rem(my_snap + step, half_count) for step in range(1, half_count)]
    far = [(1 - my_half) * half_count + lax.rem(my_snap + step, half_count) for step in range(half_count)]

    barrier = pltpu.get_barrier_semaphore()
    for peer in near + far:
        pl.semaphore_signal(barrier, inc=1, device_id=(peer, my_cell), device_id_type=MESH)
    pl.semaphore_wait(barrier, snap_count - 1)

    def columns(chunk, owner):
        return pressure_ref.at[:, pl.ds(pl.multiple_of((chunk * snap_count + owner) * wide, wide), wide)]

    def landing(chunk, source):
        return held.at[chunk, pl.ds(pl.multiple_of(source * row_count, 8), row_count)]

    def sending(chunk, peer):
        return pltpu.make_async_remote_copy(
            src_ref=columns(chunk, peer),
            dst_ref=landing(chunk, my_snap),
            send_sem=send_sem.at[chunk, peer],
            recv_sem=recv_sem.at[chunk, my_snap],
            device_id=(peer, my_cell),
            device_id_type=MESH,
        )

    def arriving(chunk, peer):
        return pltpu.make_async_remote_copy(
            src_ref=columns(chunk, peer),
            dst_ref=landing(chunk, peer),
            send_sem=send_sem.at[chunk, peer],
            recv_sem=recv_sem.at[chunk, peer],
            device_id=(peer, my_cell),
            device_id_type=MESH,
        )

    def keeping(chunk):
        return pltpu.make_async_copy(columns(chunk, my_snap), landing(chunk, my_snap), own_sem.at[chunk])

    for chunk in range(chunks):
        for peer in near:
            sending(chunk, peer).start()
        keeping(chunk).start()
    for chunk in range(chunks):
        for peer in far:
            sending(chunk, peer).start()

    table = make_table(bins_ref[...]).T
    coarse = table.astype(jnp.bfloat16)
    rows_out = 2 * kept_count
    table_parts[:rows_out] = coarse
    table_parts[rows_out:] = (table - coarse.astype(jnp.float32)).astype(jnp.bfloat16)

    half_rows = snap_count * row_count // 2
    low_count = (half_rows - NFFT) // half_len + 1
    high_start = -(-half_rows // half_len)
    assert low_count == blocks - high_start

    def transform(chunk, first, count):
        def spread(block, width):
            data = jnp.concatenate(
                [held[chunk, pl.ds(pl.multiple_of((block + i) * half_len, half_len), NFFT), :] for i in range(width)], 1
            )
            data_coarse = data.astype(jnp.bfloat16)
            data_fine = (data - data_coarse.astype(jnp.float32)).astype(jnp.bfloat16)
            both = jnp.dot(table_parts[...], data_coarse, preferred_element_type=jnp.float32)
            rest = jnp.dot(table_parts[:rows_out], data_fine, preferred_element_type=jnp.float32)
            result = both[:rows_out] + (both[rows_out:] + rest)
            for i in range(width):
                spectra[pl.ds(block + i, rows_out, stride=blocks), :] = result[:, i * wide:(i + 1) * wide]

        repeat(count // 2, 2, lambda step: spread(first + 2 * step, 2))
        if count % 2:
            spread(first + count - 1, 1)

    def product(k):
        data = jnp.concatenate(
            [spectra[pl.ds(pl.multiple_of((k + part * kept_count) * blocks, blocks), blocks), :] for part in range(2)], 0
        )
        data_coarse = data.astype(jnp.bfloat16)
        data_fine = (data - data_coarse.astype(jnp.float32)).astype(jnp.bfloat16)
        right = jnp.concatenate([data_coarse, data_fine], 0)
        both = lax.dot_general(data_coarse, right, (((1,), (1,)), ((), ())), preferred_element_type=jnp.float32)
        cross = both[:, 2 * blocks:]
        return both[:, :2 * blocks] + (cross + cross.T)

    def complex_gram(k):
        whole = grams[k] + product(k) if chunks > 1 else product(k)
        top, turned = whole[:blocks], pltpu.roll(whole[blocks:], blocks, 1)
        lane = lax.broadcasted_iota(jnp.int32, top.shape, 1)
        return jnp.where(lane < blocks, top + turned, top - turned)

    for chunk in range(chunks):
        keeping(chunk).wait()
        for peer in near:
            arriving(chunk, peer).wait_recv()
        transform(chunk, my_half * high_start, low_count)
        for peer in far:
            arriving(chunk, peer).wait_recv()
        transform(chunk, low_count, high_start - low_count)
        transform(chunk, (1 - my_half) * high_start, low_count)
        if chunk < chunks - 1:
            def accumulate(k, chunk=chunk):
                grams[k] = product(k) if chunk == 0 else grams[k] + product(k)

            repeat(kept_count, 4, accumulate)

    pairs = kept_count // snap_count // 2

    def finish(place):
        k = place // pairs * (2 * pairs) + lax.rem(place, pairs)
        first, second = complex_gram(k), complex_gram(k + pairs)
        row = lax.broadcasted_iota(jnp.int32, first.shape, 0)
        lane = lax.broadcasted_iota(jnp.int32, first.shape, 1)
        left = jnp.where(row >= lane, first, pltpu.roll(first, blocks, 1))
        right = jnp.where(row >= lane - blocks, pltpu.roll(second, blocks, 1), second)
        return jnp.where(lane < blocks, left, right)

    def write(place):
        out_ref[place] = finish(place)

    repeat(kept_count // 2, 2, write)
    for chunk in range(chunks):
        for peer in near + far:
            sending(chunk, peer).wait_send()


def local_grams(pressure, retained_bins, snap_count, blocks):
    row_count, width_local = pressure.shape
    wide = LANES
    chunks = width_local // snap_count // wide
    kept_count = retained_bins.shape[0]
    whole_vmem = pl.BlockSpec(memory_space=pltpu.VMEM)
    return pl.pallas_call(
        functools.partial(gather_kernel, snap_count, chunks, wide, kept_count, blocks),
        out_shape=jax.ShapeDtypeStruct((kept_count // 2, blocks, 2 * blocks), jnp.float32),
        in_specs=[pl.BlockSpec(memory_space=pl.ANY), whole_vmem],
        out_specs=whole_vmem,
        scratch_shapes=[
            pltpu.VMEM((chunks, snap_count * row_count, wide), jnp.float32),
            pltpu.VMEM((2 * kept_count * blocks, wide), jnp.float32),
            pltpu.VMEM((kept_count, 2 * blocks, 2 * blocks), jnp.float32),
            pltpu.VMEM((4 * kept_count, NFFT), jnp.bfloat16),
            pltpu.SemaphoreType.DMA((chunks,)),
            pltpu.SemaphoreType.DMA((chunks, snap_count)),
            pltpu.SemaphoreType.DMA((chunks, snap_count)),
        ],
        compiler_params=pltpu.CompilerParams(collective_id=1, has_side_effects=True),
    )(pressure, retained_bins.reshape(1, kept_count))


def reduce_kernel(snap_count, cell_count, scale, gram_ref, out_ref, cell_slots, own_cells, snap_slots, own_part, gathered,
                  cell_send, cell_recv, snap_send, snap_recv, gather_send, gather_recv):
    my_snap, my_cell = lax.axis_index("snap"), lax.axis_index("cell")

    def cell_peer(step):
        return lax.rem(my_cell + step, cell_count)

    def snap_peer(step):
        return lax.rem(my_snap + step, snap_count)

    barrier = pltpu.get_barrier_semaphore()
    for step in range(1, cell_count):
        pl.semaphore_signal(barrier, inc=1, device_id=(my_snap, cell_peer(step)), device_id_type=MESH)
    for step in range(1, snap_count):
        pl.semaphore_signal(barrier, inc=1, device_id=(snap_peer(step), my_cell), device_id_type=MESH)
    pl.semaphore_wait(barrier, cell_count + snap_count - 2)

    scatters = [
        pltpu.make_async_remote_copy(
            src_ref=gram_ref.at[:, cell_peer(step)],
            dst_ref=cell_slots.at[step - 1],
            send_sem=cell_send.at[step - 1],
            recv_sem=cell_recv.at[step - 1],
            device_id=(my_snap, cell_peer(step)),
            device_id_type=MESH,
        )
        for step in range(1, cell_count)
    ]
    for copy in scatters:
        copy.start()
    total = gram_ref[:, my_cell]
    for step in range(1, cell_count):
        scatters[step - 1].wait_recv()
        total = total + cell_slots[step - 1]
    own_cells[...] = total

    exchanges = [
        pltpu.make_async_remote_copy(
            src_ref=own_cells.at[snap_peer(step)],
            dst_ref=snap_slots.at[step - 1],
            send_sem=snap_send.at[step - 1],
            recv_sem=snap_recv.at[step - 1],
            device_id=(snap_peer(step), my_cell),
            device_id_type=MESH,
        )
        for step in range(1, snap_count)
    ]
    for copy in exchanges:
        copy.start()
    part = own_cells[my_snap]
    for step in range(1, snap_count):
        exchanges[step - 1].wait_recv()
        part = part + snap_slots[step - 1]
    own_part[...] = part * scale

    gathers = [
        pltpu.make_async_remote_copy(
            src_ref=own_part,
            dst_ref=gathered.at[my_cell],
            send_sem=gather_send.at[step - 1],
            recv_sem=gather_recv.at[step - 1],
            device_id=(my_snap, cell_peer(step)),
            device_id_type=MESH,
        )
        for step in range(1, cell_count)
    ]
    for copy in gathers:
        copy.start()
    out_ref[my_cell] = own_part[...]
    for step in range(1, cell_count):
        gathers[step - 1].wait_recv()
        source = lax.rem(my_cell + cell_count - step, cell_count)
        out_ref[source] = gathered[source]
    for copy in scatters + exchanges + gathers:
        copy.wait_send()


def reduce_grams(packed, scale):
    snap_count, cell_count, rows, lanes = packed.shape
    whole_vmem = pl.BlockSpec(memory_space=pltpu.VMEM)
    return pl.pallas_call(
        functools.partial(reduce_kernel, snap_count, cell_count, scale),
        out_shape=jax.ShapeDtypeStruct((cell_count, rows, lanes), jnp.float32),
        in_specs=[whole_vmem],
        out_specs=whole_vmem,
        scratch_shapes=[
            pltpu.VMEM((cell_count - 1, snap_count, rows, lanes), jnp.float32),
            pltpu.VMEM((snap_count, rows, lanes), jnp.float32),
            pltpu.VMEM((snap_count - 1, rows, lanes), jnp.float32),
            pltpu.VMEM((rows, lanes), jnp.float32),
            pltpu.VMEM((cell_count, rows, lanes), jnp.float32),
            pltpu.SemaphoreType.DMA((cell_count - 1,)),
            pltpu.SemaphoreType.DMA((cell_count - 1,)),
            pltpu.SemaphoreType.DMA((snap_count - 1,)),
            pltpu.SemaphoreType.DMA((snap_count - 1,)),
            pltpu.SemaphoreType.DMA((cell_count - 1,)),
            pltpu.SemaphoreType.DMA((cell_count - 1,)),
        ],
        compiler_params=pltpu.CompilerParams(collective_id=0, has_side_effects=True),
    )(packed)


def on_device(pressure, block_starts, retained_bins):
    snap_count = lax.axis_size("snap")
    row_count, width_local = pressure.shape
    kept_count = retained_bins.shape[0]
    blocks = block_starts.shape[0]
    lower = jnp.arange(blocks)[:, None] >= jnp.arange(blocks)[None, :]
    cell_count = lax.axis_size("cell")
    pairs = kept_count // snap_count // 2
    if pairs * blocks % (8 * cell_count) == 0 and width_local // snap_count // LANES > 1:
        return pipelined_grams(pressure, block_starts, retained_bins, snap_count, cell_count, blocks)
    halves = local_grams(pressure, retained_bins, snap_count, blocks)
    packed = halves.reshape(snap_count, cell_count, pairs * blocks // cell_count, 2 * blocks)
    reduced = reduce_grams(packed, 1.0 / (width_local * cell_count))
    paired = reduced.reshape(pairs, blocks, 2 * blocks)
    joined = jnp.concatenate([paired[:, :, :blocks], paired[:, :, blocks:]], 0)
    mirrored = joined.transpose(0, 2, 1)
    diagonal = jnp.eye(blocks, dtype=bool)
    own_real = jnp.where(lower, joined, mirrored)
    own_imag = jnp.where(diagonal, 0.0, jnp.where(lower, -mirrored, joined))
    own_block = jnp.stack([own_real, own_imag], 1)
    order = (block_starts[:, None] // (NFFT // 2) == jnp.arange(blocks)[None, :]).astype(jnp.float32)
    turned = jnp.einsum("kpij,dj->kpid", own_block, order, precision=lax.Precision.HIGHEST)
    return jnp.einsum("bi,kpid->kpbd", order, turned, precision=lax.Precision.HIGHEST)


def solution(mesh):
    placed = (P("snap", "cell"), P(), P())
    return jax.shard_map(
        on_device,
        mesh=mesh,
        in_specs=placed,
        out_specs=P("snap", None, None, None),
        check_vma=False,
    )
```

```python
import functools

import jax
import jax.numpy as jnp
from jax import lax
from jax.experimental import pallas as pl
from jax.experimental.pallas import tpu as pltpu
from jax.sharding import PartitionSpec as P

NFFT = 256
LANES = 128
AHEAD = 3
MESH = pl.DeviceIdType.MESH


def make_table(bins):
    offsets = lax.broadcasted_iota(jnp.int32, (NFFT, bins.shape[1]), 0)
    window = 0.5 - 0.5 * jnp.cos(2.0 * jnp.pi * offsets.astype(jnp.float32) / NFFT)
    norm_factor = 1.0 / jnp.sqrt(jnp.sum(window * window, axis=0, keepdims=True))
    phase_steps = (bins * offsets) & (NFFT - 1)
    angles = 2.0 * jnp.pi * phase_steps.astype(jnp.float32) / NFFT
    return jnp.concatenate([window * norm_factor * jnp.cos(angles), -window * norm_factor * jnp.sin(angles)], 1)


def repeat(count, unroll, step):
    def body(turn, carry):
        for extra in range(unroll):
            step(turn * unroll + extra)
        return carry

    lax.fori_loop(0, count // unroll, body, 0)
    for rest in range(count // unroll * unroll, count):
        step(rest)


def pipeline_kernel(snap_count, cell_count, chunks, wide, kept_count, blocks, scale, pressure_ref, index_ref, out_ref, held, half_held,
                    spectra, half_spectra, landed, grams, table_rows, table_parts, turns, sides, packed, cell_slots, own_cells, near_slots, lent_slots, far_sums, far_slot, own_part,
                    gathered, late_slots, own_sem, send_sem, recv_sem, half_own, half_send, half_recv, halo_send, halo_recv, keep_sem,
                    spec_send, spec_recv, cell_send, cell_recv, near_send, near_recv, lent_send, lent_recv, forward_send, forward_recv,
                    gather_send, gather_recv, late_send, late_recv, line_sem, flip_sem):
    my_snap, my_cell = lax.axis_index("snap"), lax.axis_index("cell")
    row_count = pressure_ref.shape[0]
    half_count = snap_count // 2
    my_half = my_snap // half_count
    half_start = my_half * half_count
    half_len = NFFT // 2
    half_rows = half_count * row_count
    half_blocks = blocks // 2
    halo = half_rows % half_len
    last = chunks - 1
    rows_out = 2 * kept_count
    groups = kept_count // snap_count // 2
    group_rows = 4 * half_blocks
    early_rows = groups * blocks // cell_count
    near = [half_start + lax.rem(my_snap + step, half_count) for step in range(1, half_count)]
    far = [half_count - my_half + step * (1 - 2 * my_half) for step in range(half_count)]
    others = near + far
    outer = my_half * (snap_count - 1)
    at_end = my_snap == outer

    def cell_peer(step):
        return lax.rem(my_cell + step, cell_count)

    bits = cell_count.bit_length() - 1

    def cell_flip(bit):
        return my_cell + 2 ** bit * (1 - 2 * lax.rem(my_cell // 2 ** bit, 2))

    def along(step):
        pl.when(my_snap > 0)(lambda: step(my_snap - 1, 1))
        pl.when(my_snap < snap_count - 1)(lambda: step(my_snap + 1, 0))

    barrier = pltpu.get_barrier_semaphore()
    along(lambda snap, side: pl.semaphore_signal(barrier, inc=1, device_id=(snap, my_cell), device_id_type=MESH))
    for bit in range(bits):
        pl.semaphore_signal(barrier, inc=1, device_id=(my_snap, cell_flip(bit)), device_id_type=MESH)
    pl.semaphore_wait(barrier, bits + jnp.minimum(my_snap, 1) + jnp.minimum(snap_count - 1 - my_snap, 1))

    def remote(source, target, send, recv, snap, cell):
        return pltpu.make_async_remote_copy(
            src_ref=source, dst_ref=target, send_sem=send, recv_sem=recv, device_id=(snap, cell), device_id_type=MESH
        )

    def columns(chunk, owner):
        return pl.ds(pl.multiple_of((chunk * snap_count + owner) * wide, wide), wide)

    def rows_of(source):
        return pl.ds(pl.multiple_of(source * row_count, 8), row_count)

    def sending(chunk, peer):
        return remote(pressure_ref.at[:, columns(chunk, peer)], held.at[chunk, rows_of(my_snap)],
                      send_sem.at[chunk, peer], recv_sem.at[chunk, my_snap], peer, my_cell)

    def arriving(chunk, peer):
        return remote(pressure_ref.at[:, columns(chunk, peer)], held.at[chunk, rows_of(peer)],
                      send_sem.at[chunk, peer], recv_sem.at[chunk, peer], peer, my_cell)

    def keeping(chunk):
        return pltpu.make_async_copy(pressure_ref.at[:, columns(chunk, my_snap)], held.at[chunk, rows_of(my_snap)], own_sem.at[chunk])

    def half_columns(peer, side):
        return columns(last, lax.rem(peer, half_count) + side * half_count)

    def half_place(source):
        return pl.ds(pl.multiple_of(my_half * halo + lax.rem(source, half_count) * row_count, 8), row_count)

    def half_sending(peer, side):
        return remote(pressure_ref.at[:, half_columns(peer, side)], half_held.at[side, half_place(my_snap)],
                      half_send.at[peer, side], half_recv.at[my_snap, side], peer, my_cell)

    def half_arriving(peer, side):
        return remote(pressure_ref.at[:, half_columns(my_snap, side)], half_held.at[side, half_place(peer)],
                      half_send.at[peer, side], half_recv.at[peer, side], peer, my_cell)

    def half_keeping(side):
        return pltpu.make_async_copy(pressure_ref.at[:, half_columns(my_snap, side)], half_held.at[side, half_place(my_snap)],
                                     half_own.at[side])

    def halo_sending(peer, side, half):
        first, place = (row_count - halo, 0) if half == 0 else (0, half_rows)
        return remote(pressure_ref.at[pl.ds(first, halo), half_columns(peer, side)], half_held.at[side, pl.ds(place, halo)],
                      halo_send.at[peer, side], halo_recv.at[side], peer, my_cell)

    def spectra_rows(owner, group):
        return pl.ds(pl.multiple_of((owner * groups + group) * group_rows, group_rows), group_rows)

    def spectra_sending(group, peer):
        return remote(half_spectra.at[:, spectra_rows(peer, group)], landed.at[my_snap, :, pl.ds(group * group_rows, group_rows)],
                      spec_send.at[group, peer], spec_recv.at[group, my_snap], peer, my_cell)

    def spectra_arriving(group, peer):
        return remote(half_spectra.at[:, spectra_rows(peer, group)], landed.at[peer, :, pl.ds(group * group_rows, group_rows)],
                      spec_send.at[group, peer], spec_recv.at[group, peer], peer, my_cell)

    def spectra_keeping():
        own = pl.ds(pl.multiple_of(my_snap * groups * group_rows, group_rows), groups * group_rows)
        return pltpu.make_async_copy(half_spectra.at[:, own], landed.at[my_snap], keep_sem.at[0])

    def at_middle(half, step):
        @pl.when(my_snap == half_count - 1 + half)
        def _():
            for peer in far:
                for side in range(2):
                    step(halo_sending(peer, side, half))

    at_cut = my_snap == half_count - 1 + my_half

    @pl.when(at_cut)
    def _():
        sending(0, far[0]).start()

    for turn in range(snap_count - 2):
        along(lambda snap, side, turn=turn: pl.semaphore_signal(
            line_sem.at[turn, side], inc=1, device_id=(snap, my_cell), device_id_type=MESH))
        along(lambda snap, side, turn=turn: pl.semaphore_wait(line_sem.at[turn, 1 - side], 1))
    for bit in range(bits):
        pl.semaphore_signal(flip_sem.at[bit], inc=1, device_id=(my_snap, cell_flip(bit)), device_id_type=MESH)
        pl.semaphore_wait(flip_sem.at[bit], 1)

    for half in range(2):
        at_middle(half, lambda copy: copy.start())
    for side in range(2):
        for peer in near:
            half_sending(peer, side).start()
        half_keeping(side).start()
    for chunk in range(last):
        for peer in near:
            sending(chunk, peer).start()
        keeping(chunk).start()
    def send_far(begun):
        for chunk in range(last):
            for peer in far[begun if chunk == 0 else 0:]:
                sending(chunk, peer).start()

    pl.when(at_cut)(lambda: send_far(1))

    table = make_table(index_ref[:1, :kept_count]).T
    for side in range(NFFT // LANES):
        for part in range(2):
            for slot in range(2 * snap_count):
                first = part * kept_count + slot * groups
                place = slot // 2 * 4 * groups + slot % 2 * 2 + part
                table_rows[side, pl.ds(place, groups, stride=4), :] = table[first:first + groups, side * LANES:(side + 1) * LANES]
    table = jnp.concatenate([table_rows[side] for side in range(NFFT // LANES)], 1)
    coarse = table.astype(jnp.bfloat16)
    table_parts[:rows_out] = coarse
    table_parts[rows_out:] = (table - coarse.astype(jnp.float32)).astype(jnp.bfloat16)

    lanes = 2 * blocks
    starts = jnp.concatenate([index_ref[1:, :blocks]] * 2, 1).astype(jnp.float32)
    across = jnp.broadcast_to(starts, (lanes, lanes))
    down = across.T
    sides[0] = down
    sides[1] = across
    row = lax.broadcasted_iota(jnp.int32, (lanes, lanes), 0)
    lane = lax.broadcasted_iota(jnp.int32, (lanes, lanes), 1)
    same_side = (row < blocks) == (lane < blocks)
    row_slot = (half_len * jnp.where(row < blocks, row, row - blocks)).astype(jnp.float32)
    lane_slot = (half_len * jnp.where(lane < blocks, lane, lane - blocks)).astype(jnp.float32)
    turns[0] = jnp.where(same_side & (down == lane_slot), 1.0, 0.0).astype(jnp.bfloat16)
    turns[1] = jnp.where(same_side & (across == row_slot), 1.0, 0.0).astype(jnp.bfloat16)

    def split(data):
        coarse = data.astype(jnp.bfloat16)
        return coarse, (data - coarse.astype(jnp.float32)).astype(jnp.bfloat16)

    def thirds(data):
        coarse, rest = split(data)
        middle = data - coarse.astype(jnp.float32)
        return [coarse, rest, (middle - rest.astype(jnp.float32)).astype(jnp.bfloat16)]

    def reorder(tile):
        left = jnp.dot(turns[0, :blocks, :blocks], jnp.concatenate(thirds(tile), 1), preferred_element_type=jnp.float32)
        tile = (left[:, :lanes] + left[:, lanes:2 * lanes]) + left[:, 2 * lanes:]
        right = jnp.dot(jnp.concatenate(thirds(tile), 0), turns[1], preferred_element_type=jnp.float32)
        return (right[:blocks] + right[blocks:2 * blocks]) + right[2 * blocks:]

    def waves(windows):
        data_coarse, data_fine = split(jnp.concatenate(windows, 1))
        both = jnp.dot(table_parts[...], data_coarse, preferred_element_type=jnp.float32)
        rest = jnp.dot(table_parts[:rows_out], data_fine, preferred_element_type=jnp.float32)
        result = both[:rows_out] + (both[rows_out:] + rest)
        return [result[:, i * wide:(i + 1) * wide] for i in range(len(windows))]

    def window_rows(block):
        return pl.ds(pl.multiple_of(block * half_len, half_len), NFFT)

    def transform(chunk, first, count):
        def spread(block, width):
            results = waves([held[chunk, window_rows(block + i), :] for i in range(width)])
            for i, result in enumerate(results):
                spectra[pl.ds(block + i, rows_out, stride=blocks), :] = result

        repeat(count // 2, 2, lambda step: spread(first + 2 * step, 2))
        if count % 2:
            spread(first + count - 1, 1)

    def half_transform(block):
        results = waves([half_held[side, window_rows(block), :] for side in range(2)])
        for side, result in enumerate(results):
            half_spectra[side, pl.ds(block, rows_out, stride=half_blocks), :] = result

    for side in range(2):
        half_keeping(side).wait()
        for peer in near:
            half_arriving(peer, side).wait_recv()
        halo_sending(my_snap, side, 0).wait_recv()
    repeat(half_blocks, 2, half_transform)
    spectra_keeping().start()

    for peer in near:
        for group in range(groups):
            spectra_sending(group, peer).start()
    pl.when(jnp.logical_not(at_cut))(lambda: send_far(0))

    def send_spectra(group):
        for peer in reversed(far):
            spectra_sending(group, peer).start()

    for group in range(min(AHEAD, groups)):
        send_spectra(group)

    def raw_product(data):
        data_coarse, data_fine = split(data)
        right = jnp.concatenate([data_coarse, data_fine], 0)
        return lax.dot_general(data_coarse, right, (((1,), (1,)), ((), ())), preferred_element_type=jnp.float32)

    def gram_product(data):
        return symmetric(raw_product(data))

    def symmetric(both):
        cross = both[:, 2 * blocks:]
        return both[:, :2 * blocks] + (cross + cross.T)

    def chunk_product(place):
        return gram_product(spectra[pl.ds(pl.multiple_of(place * 2 * blocks, 2 * blocks), 2 * blocks), :])

    def complex_gram(whole):
        top, turned = whole[:blocks], pltpu.roll(whole[blocks:], blocks, 1)
        lane = lax.broadcasted_iota(jnp.int32, top.shape, 1)
        return jnp.where(lane < blocks, top + turned, top - turned)

    def pair_up(first, second):
        first, second = complex_gram(first), complex_gram(second)
        row = lax.broadcasted_iota(jnp.int32, first.shape, 0)
        lane = lax.broadcasted_iota(jnp.int32, first.shape, 1)
        left = jnp.where(row >= lane, first, pltpu.roll(first, blocks, 1))
        right = jnp.where(row >= lane - blocks, pltpu.roll(second, blocks, 1), second)
        return jnp.where(lane < blocks, left, right)

    high_start = -(-half_rows // half_len)
    low_count = (half_rows - NFFT) // half_len + 1
    for chunk in range(last):
        keeping(chunk).wait()
        for peer in near:
            arriving(chunk, peer).wait_recv()
        transform(chunk, my_half * high_start, low_count)
        for peer in far:
            arriving(chunk, peer).wait_recv()
        if chunk == last - 1:
            for group in range(AHEAD, min(2 * AHEAD, groups)):
                send_spectra(group)
        transform(chunk, low_count, high_start - low_count)
        transform(chunk, (1 - my_half) * high_start, low_count)
        if chunk < last - 1:
            def accumulate(place, chunk=chunk):
                grams[place] = chunk_product(place) if chunk == 0 else grams[place] + chunk_product(place)

            repeat(kept_count, 4, accumulate)

    def early_gram(place):
        return grams[place] + chunk_product(place) if last > 1 else chunk_product(place)

    def early_pack(pair):
        packed[pl.ds(pl.multiple_of(pair * blocks, blocks), blocks)] = pair_up(early_gram(2 * pair), early_gram(2 * pair + 1))

    def early_share(owner, cell):
        return pl.ds(pl.multiple_of(owner * groups * blocks + cell * early_rows, 8), early_rows)

    def scattering(owner, step):
        return remote(packed.at[early_share(owner, cell_peer(step))], cell_slots.at[step - 1, owner],
                      cell_send.at[step - 1, owner], cell_recv.at[step - 1, owner], my_snap, cell_peer(step))

    def near_exchanging(peer):
        return remote(own_cells.at[peer], near_slots.at[lax.rem(my_snap, half_count)], near_send.at[peer],
                      near_recv.at[lax.rem(my_snap, half_count)], peer, my_cell)

    def near_exchanged(peer):
        return remote(own_cells.at[peer], near_slots.at[lax.rem(peer, half_count)], near_send.at[peer],
                      near_recv.at[lax.rem(peer, half_count)], peer, my_cell)

    def lending(source):
        place = lax.rem(source, half_count)
        return remote(own_cells.at[pl.ds(half_count - half_start, half_count)], lent_slots.at[place], lent_send.at[0],
                      lent_recv.at[place], outer, my_cell)

    def forwarding(peer):
        return remote(far_sums.at[lax.rem(peer, half_count)], far_slot, forward_send.at[peer], forward_recv.at[0], peer, my_cell)

    def gather_rows(cell):
        return pl.ds(pl.multiple_of(cell * early_rows, 8), early_rows)

    def gathering(step):
        return remote(own_part, gathered.at[gather_rows(my_cell)], gather_send.at[step - 1], gather_recv.at[my_cell], my_snap, cell_peer(step))

    def gather_arriving(step):
        return remote(own_part, gathered.at[gather_rows(cell_peer(step))], gather_send.at[step - 1], gather_recv.at[cell_peer(step)],
                      my_snap, cell_peer(step))

    for owner in range(snap_count):
        repeat(groups, 2, lambda pair, owner=owner: early_pack(owner * groups + pair))
        for step in range(1, cell_count):
            scattering(owner, step).start()

    def early_exchange():
        for owner in range(snap_count):
            total = packed[early_share(owner, my_cell)]
            for step in range(1, cell_count):
                scattering(owner, step).wait_recv()
                total = total + cell_slots[step - 1, owner]
            own_cells[owner] = total
        for peer in near:
            near_exchanging(peer).start()
        pl.when(jnp.logical_not(at_end))(lambda: lending(my_snap).start())

    def early_forward():
        @pl.when(at_end)
        def _():
            total = own_cells[pl.ds(half_count - half_start, half_count)]
            for peer in near:
                lending(peer).wait_recv()
                total = total + lent_slots[lax.rem(peer, half_count)]
            far_sums[...] = total
            for peer in far:
                forwarding(peer).start()

    def early_gather():
        part = own_cells[my_snap]
        for peer in near:
            near_exchanged(peer).wait_recv()
            part = part + near_slots[lax.rem(peer, half_count)]
        forwarding(my_snap).wait_recv()
        part = part + far_slot[...]
        own_part[...] = part
        for step in range(1, cell_count):
            gathering(step).start()
        gathered[gather_rows(my_cell)] = part

    def early_collect():
        for step in range(1, cell_count):
            gather_arriving(step).wait_recv()

    def late_product(group, member, place):
        sides = []
        for side in range(2):
            rows = [
                landed[half * half_count + place, side, pl.ds(group * group_rows + (2 * member + part) * half_blocks, half_blocks), :]
                for part in range(2)
                for half in range(2)
            ]
            sides.append(jnp.concatenate(rows, 0))
        return raw_product(jnp.concatenate(sides, 1))

    def late_sending(group, step):
        return remote(late_slots.at[group, my_cell], late_slots.at[group, my_cell], late_send.at[group, step - 1],
                      late_recv.at[group, my_cell], my_snap, cell_peer(step))

    def late_arriving(group, step):
        return remote(late_slots.at[group, my_cell], late_slots.at[group, cell_peer(step)], late_send.at[group, step - 1],
                      late_recv.at[group, cell_peer(step)], my_snap, cell_peer(step))

    def late_share(group):
        for peer in near:
            spectra_arriving(group, peer).wait_recv()
        grams_here = [0.0, 0.0]
        for peer in reversed(far):
            spectra_arriving(group, peer).wait_recv()
            if peer is far[-1] and 2 * AHEAD <= group + AHEAD < groups:
                send_spectra(group + AHEAD)
            for member in range(2):
                grams_here[member] += late_product(group, member, lax.rem(peer, half_count))
        late_slots[group, my_cell] = pair_up(symmetric(grams_here[0]), symmetric(grams_here[1]))
        for step in range(1, cell_count):
            late_sending(group, step).start()

    def late_sum(group):
        for step in range(1, cell_count):
            late_arriving(group, step).wait_recv()
        total = late_slots[group, 0]
        for cell in range(1, cell_count):
            total = total + late_slots[group, cell]
        total = (total + gathered[pl.ds(group * blocks, blocks)]) * scale
        tile = reorder(total)
        turned = tile.T
        rolled = pltpu.roll(tile, blocks, 1)
        before, after = sides[0, :blocks, :blocks], sides[1, :blocks, :blocks]
        for member in range(2):
            straight = (tile if member == 0 else rolled)[:, :blocks]
            mirrored = turned[member * blocks:(member + 1) * blocks]
            place = member * groups + group
            out_ref[place, 0] = jnp.where(before >= after, straight, mirrored)
            out_ref[place, 1] = jnp.where(before == after, 0.0, jnp.where(before >= after, -mirrored, straight))

    spectra_keeping().wait()
    def finish_late(done):
        for group in done:
            for peer in far:
                spectra_sending(group, peer).wait_send()
            for step in range(1, cell_count):
                late_sending(group, step).wait_send()

    def finish_early():
        for half in range(2):
            at_middle(half, lambda copy: copy.wait_send())
        for peer in near:
            for side in range(2):
                half_sending(peer, side).wait_send()
            for group in range(groups):
                spectra_sending(group, peer).wait_send()
        for chunk in range(last):
            for peer in others:
                sending(chunk, peer).wait_send()
        for step in range(1, cell_count):
            gathering(step).wait_send()
            for owner in range(snap_count):
                scattering(owner, step).wait_send()
        for peer in near:
            near_exchanging(peer).wait_send()
        pl.when(jnp.logical_not(at_end))(lambda: lending(my_snap).wait_send())

        @pl.when(at_end)
        def _():
            for peer in far:
                forwarding(peer).wait_send()

    ended = max(groups - 2, 0)
    ready = min(5, groups - 1)
    steps = {}
    for turn, step in ((0, early_exchange), (1, early_forward), (3, early_gather), (ready, early_collect)):
        steps.setdefault(min(turn, groups - 1), []).append(step)
    for group in range(groups):
        late_share(group)
        for step in steps.get(group, []):
            step()
        if group >= ready:
            for done in range(0 if group == ready else group - 1, group):
                late_sum(done)
        if group == max(groups - 2, 0):
            finish_late(range(ended))
        if group == max(groups - 2, ready):
            finish_early()
    finish_late(range(ended, groups - 1))
    late_sum(groups - 1)
    finish_late([groups - 1])


def pipelined_grams(pressure, block_starts, retained_bins, snap_count, cell_count, blocks):
    row_count, width_local = pressure.shape
    wide = LANES
    chunks = width_local // snap_count // wide
    kept_count = retained_bins.shape[0]
    groups = kept_count // snap_count // 2
    early_rows = groups * blocks // cell_count
    lanes = 2 * blocks
    half_len = NFFT // 2
    half_rows = snap_count // 2 * row_count
    halo = half_rows % half_len
    assert kept_count == blocks and cell_count & (cell_count - 1) == 0 and snap_count > 2
    assert halo == half_len // 2 and halo <= row_count and blocks % 2 == 0 and snap_count % 2 == 0
    whole_vmem = pl.BlockSpec(memory_space=pltpu.VMEM)
    scale = 1.0 / (width_local * cell_count)
    semaphores = pltpu.SemaphoreType.DMA
    return pl.pallas_call(
        functools.partial(pipeline_kernel, snap_count, cell_count, chunks, wide, kept_count, blocks, scale),
        out_shape=jax.ShapeDtypeStruct((2 * groups, 2, blocks, blocks), jnp.float32),
        in_specs=[pl.BlockSpec(memory_space=pl.ANY), whole_vmem],
        out_specs=whole_vmem,
        scratch_shapes=[
            pltpu.VMEM((chunks - 1, snap_count * row_count, wide), jnp.float32),
            pltpu.VMEM((2, half_rows + halo, wide), jnp.float32),
            pltpu.VMEM((2 * kept_count * blocks, wide), jnp.float32),
            pltpu.VMEM((2, kept_count * blocks, wide), jnp.float32),
            pltpu.VMEM((snap_count, 2, 2 * groups * blocks, wide), jnp.float32),
            pltpu.VMEM((kept_count, lanes, lanes), jnp.float32),
            pltpu.VMEM((NFFT // LANES, 2 * kept_count, LANES), jnp.float32),
            pltpu.VMEM((4 * kept_count, NFFT), jnp.bfloat16),
            pltpu.VMEM((2, lanes, lanes), jnp.bfloat16),
            pltpu.VMEM((2, lanes, lanes), jnp.float32),
            pltpu.VMEM((snap_count * groups * blocks, lanes), jnp.float32),
            pltpu.VMEM((cell_count - 1, snap_count, early_rows, lanes), jnp.float32),
            pltpu.VMEM((snap_count, early_rows, lanes), jnp.float32),
            pltpu.VMEM((snap_count // 2, early_rows, lanes), jnp.float32),
            pltpu.VMEM((snap_count // 2, snap_count // 2, early_rows, lanes), jnp.float32),
            pltpu.VMEM((snap_count // 2, early_rows, lanes), jnp.float32),
            pltpu.VMEM((early_rows, lanes), jnp.float32),
            pltpu.VMEM((early_rows, lanes), jnp.float32),
            pltpu.VMEM((groups * blocks, lanes), jnp.float32),
            pltpu.VMEM((groups, cell_count, blocks, lanes), jnp.float32),
            semaphores((chunks,)),
            semaphores((chunks, snap_count)),
            semaphores((chunks, snap_count)),
            semaphores((2,)),
            semaphores((snap_count, 2)),
            semaphores((snap_count, 2)),
            semaphores((snap_count, 2)),
            semaphores((2,)),
            semaphores((1,)),
            semaphores((groups, snap_count)),
            semaphores((groups, snap_count)),
            semaphores((cell_count - 1, snap_count)),
            semaphores((cell_count - 1, snap_count)),
            semaphores((snap_count,)),
            semaphores((snap_count // 2,)),
            semaphores((1,)),
            semaphores((snap_count // 2,)),
            semaphores((snap_count,)),
            semaphores((1,)),
            semaphores((cell_count - 1,)),
            semaphores((cell_count,)),
            semaphores((groups, cell_count - 1)),
            semaphores((groups, cell_count)),
            pltpu.SemaphoreType.REGULAR((snap_count - 2, 2)),
            pltpu.SemaphoreType.REGULAR((cell_count.bit_length() - 1,)),
        ],
        compiler_params=pltpu.CompilerParams(collective_id=2, has_side_effects=True, vmem_limit_bytes=46 * 2**20),
    )(pressure, jnp.stack([retained_bins, block_starts]))


def gather_kernel(snap_count, chunks, wide, kept_count, blocks, pressure_ref, bins_ref, out_ref, held, spectra, grams,
                  table_parts, own_sem, send_sem, recv_sem):
    my_snap, my_cell = lax.axis_index("snap"), lax.axis_index("cell")
    row_count = pressure_ref.shape[0]
    half_count = snap_count // 2
    my_half = my_snap // half_count
    half_len = NFFT // 2
    near = [my_half * half_count + lax.rem(my_snap + step, half_count) for step in range(1, half_count)]
    far = [(1 - my_half) * half_count + lax.rem(my_snap + step, half_count) for step in range(half_count)]

    barrier = pltpu.get_barrier_semaphore()
    for peer in near + far:
        pl.semaphore_signal(barrier, inc=1, device_id=(peer, my_cell), device_id_type=MESH)
    pl.semaphore_wait(barrier, snap_count - 1)

    def columns(chunk, owner):
        return pressure_ref.at[:, pl.ds(pl.multiple_of((chunk * snap_count + owner) * wide, wide), wide)]

    def landing(chunk, source):
        return held.at[chunk, pl.ds(pl.multiple_of(source * row_count, 8), row_count)]

    def sending(chunk, peer):
        return pltpu.make_async_remote_copy(
            src_ref=columns(chunk, peer),
            dst_ref=landing(chunk, my_snap),
            send_sem=send_sem.at[chunk, peer],
            recv_sem=recv_sem.at[chunk, my_snap],
            device_id=(peer, my_cell),
            device_id_type=MESH,
        )

    def arriving(chunk, peer):
        return pltpu.make_async_remote_copy(
            src_ref=columns(chunk, peer),
            dst_ref=landing(chunk, peer),
            send_sem=send_sem.at[chunk, peer],
            recv_sem=recv_sem.at[chunk, peer],
            device_id=(peer, my_cell),
            device_id_type=MESH,
        )

    def keeping(chunk):
        return pltpu.make_async_copy(columns(chunk, my_snap), landing(chunk, my_snap), own_sem.at[chunk])

    for chunk in range(chunks):
        for peer in near:
            sending(chunk, peer).start()
        keeping(chunk).start()
    for chunk in range(chunks):
        for peer in far:
            sending(chunk, peer).start()

    table = make_table(bins_ref[...]).T
    coarse = table.astype(jnp.bfloat16)
    rows_out = 2 * kept_count
    table_parts[:rows_out] = coarse
    table_parts[rows_out:] = (table - coarse.astype(jnp.float32)).astype(jnp.bfloat16)

    half_rows = snap_count * row_count // 2
    low_count = (half_rows - NFFT) // half_len + 1
    high_start = -(-half_rows // half_len)
    assert low_count == blocks - high_start

    def transform(chunk, first, count):
        def spread(block, width):
            data = jnp.concatenate(
                [held[chunk, pl.ds(pl.multiple_of((block + i) * half_len, half_len), NFFT), :] for i in range(width)], 1
            )
            data_coarse = data.astype(jnp.bfloat16)
            data_fine = (data - data_coarse.astype(jnp.float32)).astype(jnp.bfloat16)
            both = jnp.dot(table_parts[...], data_coarse, preferred_element_type=jnp.float32)
            rest = jnp.dot(table_parts[:rows_out], data_fine, preferred_element_type=jnp.float32)
            result = both[:rows_out] + (both[rows_out:] + rest)
            for i in range(width):
                spectra[pl.ds(block + i, rows_out, stride=blocks), :] = result[:, i * wide:(i + 1) * wide]

        repeat(count // 2, 2, lambda step: spread(first + 2 * step, 2))
        if count % 2:
            spread(first + count - 1, 1)

    def product(k):
        data = jnp.concatenate(
            [spectra[pl.ds(pl.multiple_of((k + part * kept_count) * blocks, blocks), blocks), :] for part in range(2)], 0
        )
        data_coarse = data.astype(jnp.bfloat16)
        data_fine = (data - data_coarse.astype(jnp.float32)).astype(jnp.bfloat16)
        right = jnp.concatenate([data_coarse, data_fine], 0)
        both = lax.dot_general(data_coarse, right, (((1,), (1,)), ((), ())), preferred_element_type=jnp.float32)
        cross = both[:, 2 * blocks:]
        return both[:, :2 * blocks] + (cross + cross.T)

    def complex_gram(k):
        whole = grams[k] + product(k) if chunks > 1 else product(k)
        top, turned = whole[:blocks], pltpu.roll(whole[blocks:], blocks, 1)
        lane = lax.broadcasted_iota(jnp.int32, top.shape, 1)
        return jnp.where(lane < blocks, top + turned, top - turned)

    for chunk in range(chunks):
        keeping(chunk).wait()
        for peer in near:
            arriving(chunk, peer).wait_recv()
        transform(chunk, my_half * high_start, low_count)
        for peer in far:
            arriving(chunk, peer).wait_recv()
        transform(chunk, low_count, high_start - low_count)
        transform(chunk, (1 - my_half) * high_start, low_count)
        if chunk < chunks - 1:
            def accumulate(k, chunk=chunk):
                grams[k] = product(k) if chunk == 0 else grams[k] + product(k)

            repeat(kept_count, 4, accumulate)

    pairs = kept_count // snap_count // 2

    def finish(place):
        k = place // pairs * (2 * pairs) + lax.rem(place, pairs)
        first, second = complex_gram(k), complex_gram(k + pairs)
        row = lax.broadcasted_iota(jnp.int32, first.shape, 0)
        lane = lax.broadcasted_iota(jnp.int32, first.shape, 1)
        left = jnp.where(row >= lane, first, pltpu.roll(first, blocks, 1))
        right = jnp.where(row >= lane - blocks, pltpu.roll(second, blocks, 1), second)
        return jnp.where(lane < blocks, left, right)

    def write(place):
        out_ref[place] = finish(place)

    repeat(kept_count // 2, 2, write)
    for chunk in range(chunks):
        for peer in near + far:
            sending(chunk, peer).wait_send()


def local_grams(pressure, retained_bins, snap_count, blocks):
    row_count, width_local = pressure.shape
    wide = LANES
    chunks = width_local // snap_count // wide
    kept_count = retained_bins.shape[0]
    whole_vmem = pl.BlockSpec(memory_space=pltpu.VMEM)
    return pl.pallas_call(
        functools.partial(gather_kernel, snap_count, chunks, wide, kept_count, blocks),
        out_shape=jax.ShapeDtypeStruct((kept_count // 2, blocks, 2 * blocks), jnp.float32),
        in_specs=[pl.BlockSpec(memory_space=pl.ANY), whole_vmem],
        out_specs=whole_vmem,
        scratch_shapes=[
            pltpu.VMEM((chunks, snap_count * row_count, wide), jnp.float32),
            pltpu.VMEM((2 * kept_count * blocks, wide), jnp.float32),
            pltpu.VMEM((kept_count, 2 * blocks, 2 * blocks), jnp.float32),
            pltpu.VMEM((4 * kept_count, NFFT), jnp.bfloat16),
            pltpu.SemaphoreType.DMA((chunks,)),
            pltpu.SemaphoreType.DMA((chunks, snap_count)),
            pltpu.SemaphoreType.DMA((chunks, snap_count)),
        ],
        compiler_params=pltpu.CompilerParams(collective_id=1, has_side_effects=True),
    )(pressure, retained_bins.reshape(1, kept_count))


def reduce_kernel(snap_count, cell_count, scale, gram_ref, out_ref, cell_slots, own_cells, snap_slots, own_part, gathered,
                  cell_send, cell_recv, snap_send, snap_recv, gather_send, gather_recv):
    my_snap, my_cell = lax.axis_index("snap"), lax.axis_index("cell")

    def cell_peer(step):
        return lax.rem(my_cell + step, cell_count)

    def snap_peer(step):
        return lax.rem(my_snap + step, snap_count)

    barrier = pltpu.get_barrier_semaphore()
    for step in range(1, cell_count):
        pl.semaphore_signal(barrier, inc=1, device_id=(my_snap, cell_peer(step)), device_id_type=MESH)
    for step in range(1, snap_count):
        pl.semaphore_signal(barrier, inc=1, device_id=(snap_peer(step), my_cell), device_id_type=MESH)
    pl.semaphore_wait(barrier, cell_count + snap_count - 2)

    scatters = [
        pltpu.make_async_remote_copy(
            src_ref=gram_ref.at[:, cell_peer(step)],
            dst_ref=cell_slots.at[step - 1],
            send_sem=cell_send.at[step - 1],
            recv_sem=cell_recv.at[step - 1],
            device_id=(my_snap, cell_peer(step)),
            device_id_type=MESH,
        )
        for step in range(1, cell_count)
    ]
    for copy in scatters:
        copy.start()
    total = gram_ref[:, my_cell]
    for step in range(1, cell_count):
        scatters[step - 1].wait_recv()
        total = total + cell_slots[step - 1]
    own_cells[...] = total

    exchanges = [
        pltpu.make_async_remote_copy(
            src_ref=own_cells.at[snap_peer(step)],
            dst_ref=snap_slots.at[step - 1],
            send_sem=snap_send.at[step - 1],
            recv_sem=snap_recv.at[step - 1],
            device_id=(snap_peer(step), my_cell),
            device_id_type=MESH,
        )
        for step in range(1, snap_count)
    ]
    for copy in exchanges:
        copy.start()
    part = own_cells[my_snap]
    for step in range(1, snap_count):
        exchanges[step - 1].wait_recv()
        part = part + snap_slots[step - 1]
    own_part[...] = part * scale

    gathers = [
        pltpu.make_async_remote_copy(
            src_ref=own_part,
            dst_ref=gathered.at[my_cell],
            send_sem=gather_send.at[step - 1],
            recv_sem=gather_recv.at[step - 1],
            device_id=(my_snap, cell_peer(step)),
            device_id_type=MESH,
        )
        for step in range(1, cell_count)
    ]
    for copy in gathers:
        copy.start()
    out_ref[my_cell] = own_part[...]
    for step in range(1, cell_count):
        gathers[step - 1].wait_recv()
        source = lax.rem(my_cell + cell_count - step, cell_count)
        out_ref[source] = gathered[source]
    for copy in scatters + exchanges + gathers:
        copy.wait_send()


def reduce_grams(packed, scale):
    snap_count, cell_count, rows, lanes = packed.shape
    whole_vmem = pl.BlockSpec(memory_space=pltpu.VMEM)
    return pl.pallas_call(
        functools.partial(reduce_kernel, snap_count, cell_count, scale),
        out_shape=jax.ShapeDtypeStruct((cell_count, rows, lanes), jnp.float32),
        in_specs=[whole_vmem],
        out_specs=whole_vmem,
        scratch_shapes=[
            pltpu.VMEM((cell_count - 1, snap_count, rows, lanes), jnp.float32),
            pltpu.VMEM((snap_count, rows, lanes), jnp.float32),
            pltpu.VMEM((snap_count - 1, rows, lanes), jnp.float32),
            pltpu.VMEM((rows, lanes), jnp.float32),
            pltpu.VMEM((cell_count, rows, lanes), jnp.float32),
            pltpu.SemaphoreType.DMA((cell_count - 1,)),
            pltpu.SemaphoreType.DMA((cell_count - 1,)),
            pltpu.SemaphoreType.DMA((snap_count - 1,)),
            pltpu.SemaphoreType.DMA((snap_count - 1,)),
            pltpu.SemaphoreType.DMA((cell_count - 1,)),
            pltpu.SemaphoreType.DMA((cell_count - 1,)),
        ],
        compiler_params=pltpu.CompilerParams(collective_id=0, has_side_effects=True),
    )(packed)


def on_device(pressure, block_starts, retained_bins):
    snap_count = lax.axis_size("snap")
    row_count, width_local = pressure.shape
    kept_count = retained_bins.shape[0]
    blocks = block_starts.shape[0]
    lower = jnp.arange(blocks)[:, None] >= jnp.arange(blocks)[None, :]
    cell_count = lax.axis_size("cell")
    pairs = kept_count // snap_count // 2
    if pairs * blocks % (8 * cell_count) == 0 and width_local // snap_count // LANES > 1:
        return pipelined_grams(pressure, block_starts, retained_bins, snap_count, cell_count, blocks)
    halves = local_grams(pressure, retained_bins, snap_count, blocks)
    packed = halves.reshape(snap_count, cell_count, pairs * blocks // cell_count, 2 * blocks)
    reduced = reduce_grams(packed, 1.0 / (width_local * cell_count))
    paired = reduced.reshape(pairs, blocks, 2 * blocks)
    joined = jnp.concatenate([paired[:, :, :blocks], paired[:, :, blocks:]], 0)
    mirrored = joined.transpose(0, 2, 1)
    diagonal = jnp.eye(blocks, dtype=bool)
    own_real = jnp.where(lower, joined, mirrored)
    own_imag = jnp.where(diagonal, 0.0, jnp.where(lower, -mirrored, joined))
    own_block = jnp.stack([own_real, own_imag], 1)
    order = (block_starts[:, None] // (NFFT // 2) == jnp.arange(blocks)[None, :]).astype(jnp.float32)
    turned = jnp.einsum("kpij,dj->kpid", own_block, order, precision=lax.Precision.HIGHEST)
    return jnp.einsum("bi,kpid->kpbd", order, turned, precision=lax.Precision.HIGHEST)


def solution(mesh):
    placed = (P("snap", "cell"), P(), P())
    return jax.shard_map(
        on_device,
        mesh=mesh,
        in_specs=placed,
        out_specs=P("snap", None, None, None),
        check_vma=False,
    )
```
